512 devices in a mesh: ctx: 128 (over x, y, z_hi, core), tp: 4 (over z_lo).
Axes of the slice: x: 4, y: 4, z: 16 (z_hi: 4, z_lo: 4; z = z_hi * 4 + z_lo), core: 2. Of those that a mesh axis runs over, the one named last changes fastest.
Arguments:
- x_gate: bfloat16 [16384, 2048], P('ctx', 'tp'), may hold values from -6 to 6
- x_post: bfloat16 [16384, 2048], P('ctx', 'tp'), may hold values from -6 to 6
- values: bfloat16 [16384, 2048], P('ctx', 'tp'), may hold values from -6 to 6
- decay: float32 [2, 2048, 16], P(None, 'tp'), may hold values from 1.5258789e-05 to 0.05
- residue: float32 [2, 2048, 16], P(None, 'tp'), may hold values from -4 to 4
- w_out: bfloat16 [2048, 2048], P(('tp', 'ctx')), may hold values from -0.125 to 0.125
Outputs:
- projected: bfloat16 [16384, 2048], P('ctx', 'tp')
The draws below stay inside these ranges and needn't reach their ends.
All inputs are finite; a program needn't handle non-finite values.
Results may differ from the reference program's by a relative error of at most 0.015.
Values may be sent and summed in bfloat16 or wider, within the bound.
A program may use at most 128 MiB of HBM per device.

```python
import jax
import jax.numpy as jnp
from jax import lax

C = 2048
DO = 2048
K = 16
SEQ = 16384


def draw_decay(key, part):
    lowest = 1.0 / (4.0 * SEQ)
    highest = 0.05
    spread = jax.random.uniform(key, (2, C, K), jnp.float32)
    return jnp.exp(jnp.log(lowest) + spread * (jnp.log(highest) - jnp.log(lowest)))


def levels(own_key, dims, shards, low, high):
    factor_of = 1.0
    for position, parts in shards:
        draws = jax.random.uniform(jax.random.fold_in(jax.random.fold_in(own_key, 6), position), (parts,), jnp.float32, low / len(shards), high / len(shards))
        factor_of = factor_of * jnp.repeat(jnp.exp(draws), dims[position] // parts).reshape((-1,) + (1,) * (len(dims) - 1 - position))
    return factor_of


def normal_values(key, dims, scale, bound, cuts=(), kind=jnp.bfloat16):
    result = jax.random.normal(key, dims, jnp.float32) * scale
    if len(cuts) > 0:
        result = levels(key, dims, cuts, -0.22, 0.18) * result
    return jnp.clip(result, min=-bound, max=bound).astype(kind)


def setup_inputs(seed: int = 0) -> dict:
    key_of = jax.random.split(jax.random.key(seed), 7)
    return {
        "x_gate": normal_values(key_of[0], (SEQ, C), 1.0, 6.0, ((0, 128), (1, 4))),
        "x_post": normal_values(key_of[1], (SEQ, C), 1.0, 6.0, ((0, 128), (1, 4))),
        "values": normal_values(key_of[2], (SEQ, C), 1.0, 6.0, ((0, 128), (1, 4))),
        "decay": draw_decay(jax.random.fold_in(key_of[6], 71), 0),
        "residue": normal_values(key_of[4], (2, C, K), 1.0, 4.0, ((1, 4),), jnp.float32),
        "w_out": normal_values(key_of[5], (DO, C), C ** -0.5, 0.125, ((0, 512),)),
    }


def kernel(decay_rows, residue_rows):
    inner_len = min(256, SEQ)
    outer_len = SEQ // inner_len
    weight = residue_rows * jnp.sqrt(2.0 * decay_rows / K)
    coarse = jnp.exp(-decay_rows[:, :, None] * (jnp.arange(outer_len, dtype=jnp.float32) * inner_len))
    fine_part = jnp.exp(-decay_rows[:, :, None] * jnp.arange(inner_len, dtype=jnp.float32))
    filter_rows = jnp.einsum('ck,ckq,ckr->cqr', weight, coarse, fine_part, precision=lax.Precision.HIGHEST)
    return filter_rows.reshape(decay_rows.shape[0], SEQ)

def spectra(signal):
    return jnp.fft.rfft(signal, n=2 * SEQ, axis=-1)

def restore(spectrum_rows):
    return jnp.fft.irfft(spectrum_rows, n=2 * SEQ, axis=-1)[:, :SEQ]

def branch(gate_rows, post_rows, value_rows, own_spec, pair_spec):
    gate_rows = gate_rows.astype(jnp.float32)
    value_spec = spectra(value_rows.astype(jnp.float32))
    along_fwd = restore(value_spec * own_spec[0])
    along_rev = restore(value_spec * jnp.conj(pair_spec[0]))
    summed = restore(spectra(gate_rows * along_fwd) * own_spec[1] + spectra(gate_rows * along_rev) * jnp.conj(pair_spec[1]))
    return (post_rows.astype(jnp.float32) * summed).astype(jnp.bfloat16)

def block_pair(block):
    gate_lo, post_lo, value_lo, gate_hi, post_hi, value_hi, rate_lo, res_lo, rate_hi, res_hi = block
    spec_lo = [spectra(kernel(rate_lo[filter_index], res_lo[filter_index])) for filter_index in range(2)]
    spec_hi = [spectra(kernel(rate_hi[filter_index], res_hi[filter_index])) for filter_index in range(2)]
    return (branch(gate_lo, post_lo, value_lo, spec_lo, spec_hi), branch(gate_hi, post_hi, value_hi, spec_hi, spec_lo))

def reference(x_gate, x_post, values, decay, residue, w_out):
    half_count = C // 2
    block_rows = 16
    blocks = half_count // block_rows

    def lower_rows(source):
        return source.T[:half_count].reshape(blocks, block_rows, SEQ)

    def upper_rows(source):
        return source.T[::-1][:half_count].reshape(blocks, block_rows, SEQ)

    def params_low(source):
        return jnp.transpose(source[:, :half_count].reshape(2, blocks, block_rows, K), (1, 0, 2, 3))

    def params_high(source):
        return jnp.transpose(source[:, ::-1][:, :half_count].reshape(2, blocks, block_rows, K), (1, 0, 2, 3))
    low_out, high_out = lax.map(block_pair, (lower_rows(x_gate), lower_rows(x_post), lower_rows(values), upper_rows(x_gate), upper_rows(x_post), upper_rows(values), params_low(decay), params_low(residue), params_high(decay), params_high(residue)))
    mixed = jnp.concatenate([low_out.reshape(half_count, SEQ), high_out.reshape(half_count, SEQ)[::-1]], axis=0).T
    return jnp.dot(mixed, w_out.T, preferred_element_type=jnp.float32).astype(jnp.bfloat16)
```

```python
import jax
import jax.numpy as jnp
from jax import lax
from jax.experimental import pallas as pl
from jax.experimental.pallas import tpu as pltpu
from jax.sharding import PartitionSpec as P

MESH = pl.DeviceIdType.MESH
F32 = jnp.float32
BF16 = jnp.bfloat16

POLES = 16
CHUNK = 128
STEPS = 16
SUBS = 8
LANES = 128
TILES = 4
GROUP = 8
PLANES = 16
TP = 4
WIDTH = TILES * LANES


def mixer_kernel(
    gate_hbm,
    post_hbm,
    vals_hbm,
    decay_hbm,
    residue_hbm,
    w_hbm,
    out_ref,
    gate_s,
    post_s,
    vals_s,
    decay_s,
    residue_s,
    w_s,
    params,
    flipped,
    rate,
    weight,
    v4,
    g4,
    p4,
    y4,
    u4,
    finals,
    inits,
    corr,
    state_out,
    state_in,
    total_out,
    total_in,
    carry_out,
    carry_in,
    w_pair,
    w_chip,
    w_planes,
    w_rows,
    w_full,
    mix_f32,
    mix,
    acc,
    load_sem,
    par_send,
    par_recv,
    st_send,
    st_recv,
    tot_send,
    tot_recv,
    car_send,
    car_recv,
    w_send,
    w_recv,
    mix_send,
    mix_recv,
):
    ctx = lax.axis_index("ctx")
    tp = lax.axis_index("tp")
    plane = ctx // GROUP
    slot = lax.rem(ctx, GROUP)
    z_hi = slot // 2
    core = lax.rem(slot, 2)
    my_dir = slot // TILES
    my_tile = lax.rem(slot, TILES)

    loads = [
        pltpu.make_async_copy(src, dst, load_sem.at[index])
        for index, (src, dst) in enumerate(
            [
                (decay_hbm, decay_s),
                (residue_hbm, residue_s),
                (vals_hbm, vals_s),
                (w_hbm, w_s),
                (gate_hbm, gate_s),
                (post_hbm, post_s),
            ]
        )
    ]
    for load in loads:
        load.start()

    barrier = pltpu.get_barrier_semaphore()
    for offset in range(1, TP):
        pl.semaphore_signal(
            barrier, inc=1, device_id={"tp": lax.rem(tp + offset, TP)}, device_id_type=MESH
        )
    for offset in range(1, GROUP):
        peer = plane * GROUP + lax.rem(slot + offset, GROUP)
        pl.semaphore_signal(barrier, inc=1, device_id={"ctx": peer}, device_id_type=MESH)
    for offset in range(1, PLANES):
        peer = lax.rem(plane + offset, PLANES) * GROUP + slot
        pl.semaphore_signal(barrier, inc=1, device_id={"ctx": peer}, device_id_type=MESH)

    row_id = lax.broadcasted_iota(jnp.int32, (LANES, 2 * LANES), 0)
    col_id = lax.broadcasted_iota(jnp.int32, (LANES, 2 * LANES), 1)
    picks = ((row_id == col_id) | (row_id + col_id == 2 * LANES - 1)).astype(F32)
    loads[0].wait()
    loads[1].wait()
    for filt in range(2):
        for which, source in enumerate((decay_s, residue_s)):
            for tile in range(TILES):
                both = lax.dot_general(
                    source[filt, tile * LANES : (tile + 1) * LANES, :],
                    picks,
                    (((0,), (0,)), ((), ())),
                    precision=lax.Precision.HIGHEST,
                    preferred_element_type=F32,
                )
                params[filt, 0, which, tile] = both[:, :LANES]
                flipped[filt, which, TILES - 1 - tile] = both[:, LANES:]
    loads[3].wait()
    w_pair[core] = w_s[...].astype(F32)

    pl.semaphore_wait(barrier, (TP - 1) + (GROUP - 1) + (PLANES - 1))

    par_copies = []
    for filt in range(2):
        copy = pltpu.make_async_remote_copy(
            src_ref=flipped.at[filt],
            dst_ref=params.at[filt, 1],
            send_sem=par_send.at[filt],
            recv_sem=par_recv.at[filt],
            device_id={"tp": TP - 1 - tp},
            device_id_type=MESH,
        )
        copy.start()
        par_copies.append(copy)
    w_core = pltpu.make_async_remote_copy(
        src_ref=w_pair.at[core],
        dst_ref=w_pair.at[core],
        send_sem=w_send.at[0],
        recv_sem=w_recv.at[0],
        device_id={"ctx": ctx + 1 - 2 * core},
        device_id_type=MESH,
    )
    w_core.start()

    def derive(filt, side):
        for tile in range(TILES):
            decay = params[filt, side, 0, tile]
            rate[filt, side, tile] = jnp.exp(-decay)
            weight[filt, side, tile] = params[filt, side, 1, tile] * jnp.sqrt(
                2.0 * decay / POLES
            )

    def row8(ref, filt, side, tile, pole):
        return jnp.broadcast_to(ref[filt, side, tile, pole : pole + 1, :], (SUBS, LANES))

    def step_order(side):
        return range(STEPS) if side == 0 else range(STEPS - 1, -1, -1)

    def sub_order(side):
        return range(SUBS) if side == 0 else range(SUBS - 1, -1, -1)

    def picked(ref, tile, step):
        return ref[tile, pl.ds(step, SUBS, stride=STEPS), :]

    def chunk_states(filt, side, tile, xs):
        order = step_order(side)
        for pole in range(POLES):
            a = row8(rate, filt, side, tile, pole)
            state = xs[order[0]]
            for step in order[1:]:
                state = a * state + xs[step]
            finals[side, pole * SUBS : (pole + 1) * SUBS, :] = state
        a_sub = jnp.exp(-float(STEPS) * params[filt, side, 0, tile])
        running = [jnp.zeros((SUBS, LANES), F32) for _ in range(2)]
        for sub in sub_order(side):
            for half in range(2):
                rows = pl.ds(half * 64 + sub, 8, stride=SUBS)
                inits[side, tile, rows, :] = running[half]
                running[half] = (
                    a_sub[half * 8 : half * 8 + 8] * running[half] + finals[side, rows, :]
                )
        for half in range(2):
            state_out[filt, side * TILES + tile, half * 8 : half * 8 + 8, :] = running[half]

    def local_output(filt, side, tile, xs, ys):
        for pole in range(POLES):
            a = row8(rate, filt, side, tile, pole)
            w = row8(weight, filt, side, tile, pole)
            state = inits[side, tile, pole * SUBS : (pole + 1) * SUBS, :]
            for step in step_order(side):
                state = a * state + xs[step]
                term = w * state
                ys[step] = term if ys[step] is None else ys[step] + term
        return ys

    def correct(filt, side, tile, ys):
        decay = params[filt, side, 0, tile]
        a_sub = jnp.exp(-float(STEPS) * decay)
        term = weight[filt, side, tile] * carry_in[filt, side * TILES + tile]
        for sub in sub_order(side):
            for half in range(2):
                corr[side, pl.ds(half * 64 + sub, 8, stride=SUBS), :] = term[
                    half * 8 : half * 8 + 8
                ]
            term = a_sub * term
        for pole in range(POLES):
            a = row8(rate, filt, side, tile, pole)
            part = corr[side, pole * SUBS : (pole + 1) * SUBS, :]
            for step in step_order(side):
                part = a * part
                ys[step] = ys[step] + part
        return ys

    def send_state(filt, index):
        @pl.when(index != slot)
        def _():
            pltpu.make_async_remote_copy(
                src_ref=state_out.at[filt, index],
                dst_ref=state_in.at[filt, slot],
                send_sem=st_send.at[filt],
                recv_sem=st_recv.at[filt],
                device_id={"ctx": plane * GROUP + index},
                device_id_type=MESH,
            ).start()

        @pl.when(index == slot)
        def _():
            state_in[filt, slot] = state_out[filt, slot]

    def wait_bytes(ref, sem):
        pltpu.make_async_copy(ref, ref, sem).wait()

    def in_order(position, count):
        return position + my_dir * (count - 1 - 2 * position)

    def group_totals(filt):
        wait_bytes(state_in.at[filt, pl.ds(0, GROUP - 1)], st_recv.at[filt])
        a_chunk = jnp.exp(-float(CHUNK) * params[filt, my_dir, 0, my_tile])
        total = state_in[filt, in_order(0, GROUP)]
        for position in range(1, GROUP):
            total = a_chunk * total + state_in[filt, in_order(position, GROUP)]
        total_out[filt] = total
        total_in[filt, plane] = total
        for offset in range(1, PLANES):
            pltpu.make_async_remote_copy(
                src_ref=total_out.at[filt],
                dst_ref=total_in.at[filt, plane],
                send_sem=tot_send.at[filt],
                recv_sem=tot_recv.at[filt],
                device_id={"ctx": lax.rem(plane + offset, PLANES) * GROUP + slot},
                device_id_type=MESH,
            ).start()

    def carries(filt):
        wait_bytes(total_in.at[filt, pl.ds(0, PLANES - 1)], tot_recv.at[filt])
        decay = params[filt, my_dir, 0, my_tile]
        a_chunk = jnp.exp(-float(CHUNK) * decay)
        a_group = jnp.exp(-float(CHUNK * GROUP) * decay)
        mine = in_order(plane, PLANES)
        carry = jnp.zeros((POLES, LANES), F32)
        for position in range(PLANES - 1):
            further = a_group * carry + total_in[filt, in_order(position, PLANES)]
            carry = jnp.where(position < mine, further, carry)
        for position in range(GROUP):
            index = in_order(position, GROUP)
            carry_out[filt, index] = carry
            carry = a_chunk * carry + state_in[filt, index]
        for offset in range(1, GROUP):
            index = lax.rem(slot + offset, GROUP)
            pltpu.make_async_remote_copy(
                src_ref=carry_out.at[filt, index],
                dst_ref=carry_in.at[filt, slot],
                send_sem=car_send.at[filt],
                recv_sem=car_recv.at[filt],
                device_id={"ctx": plane * GROUP + index},
                device_id_type=MESH,
            ).start()
        carry_in[filt, slot] = carry_out[filt, slot]

    def wait_carries(filt):
        wait_bytes(carry_in.at[filt, pl.ds(0, GROUP - 1)], car_recv.at[filt])

    def loop_tiles(body):
        def step(tile, done):
            body(tile)
            return done

        lax.fori_loop(0, TILES, step, 0)

    derive(0, 0)
    loads[2].wait()
    for tile in range(TILES):
        v4[tile] = vals_s[:, tile * LANES : (tile + 1) * LANES].astype(F32)

    def first_states(side):
        def body(tile):
            chunk_states(0, side, tile, [picked(v4, tile, step) for step in range(STEPS)])
            send_state(0, side * TILES + tile)

        return body

    loop_tiles(first_states(0))
    par_copies[0].wait_recv()
    derive(0, 1)
    loop_tiles(first_states(1))

    w_core.wait_recv()
    w_chip[0:4, :] = w_pair[0]
    w_chip[4:8, :] = w_pair[1]
    for part in range(2):
        columns = pl.ds(pl.multiple_of((2 * core + part) * WIDTH, WIDTH), WIDTH)
        w_planes[z_hi, part] = w_chip[:, columns].astype(BF16)
    for offset in range(1, 4):
        pltpu.make_async_remote_copy(
            src_ref=w_planes.at[z_hi],
            dst_ref=w_planes.at[z_hi],
            send_sem=w_send.at[1],
            recv_sem=w_recv.at[1],
            device_id={"ctx": plane * GROUP + lax.rem(z_hi + offset, 4) * 2 + core},
            device_id_type=MESH,
        ).start()

    def first_output(side):
        def body(tile):
            xs = [picked(v4, tile, step) for step in range(STEPS)]
            ys = local_output(0, side, tile, xs, [None] * STEPS)
            for step in range(STEPS):
                y4[side, tile, step] = ys[step]

        return body

    loop_tiles(first_output(0))
    group_totals(0)
    derive(1, 0)
    loads[4].wait()
    loads[5].wait()
    for tile in range(TILES):
        g4[tile] = gate_s[:, tile * LANES : (tile + 1) * LANES].astype(F32)
        p4[tile] = post_s[:, tile * LANES : (tile + 1) * LANES].astype(F32)
    loop_tiles(first_output(1))
    par_copies[1].wait_recv()
    derive(1, 1)
    carries(0)

    wait_bytes(w_planes.at[pl.ds(0, 3)], w_recv.at[1])
    for part in range(2):
        for other in range(4):
            w_rows[other * 8 : other * 8 + 8, :] = w_planes[other, part].astype(F32)
        w_full[2 * core + part, plane] = w_rows[...].astype(BF16)
    for offset in range(1, PLANES):
        pltpu.make_async_remote_copy(
            src_ref=w_full.at[pl.ds(2 * core, 2), plane],
            dst_ref=w_full.at[pl.ds(2 * core, 2), plane],
            send_sem=w_send.at[2],
            recv_sem=w_recv.at[2],
            device_id={"ctx": lax.rem(plane + offset, PLANES) * GROUP + slot},
            device_id_type=MESH,
        ).start()

    wait_carries(0)

    def second_states(tile):
        for side in range(2):
            ys = [y4[side, tile, step] for step in range(STEPS)]
            ys = correct(0, side, tile, ys)
            for step in range(STEPS):
                ys[step] = ys[step] * picked(g4, tile, step)
                u4[side, tile, step] = ys[step]
            chunk_states(1, side, tile, ys)
            send_state(1, side * TILES + tile)

    loop_tiles(second_states)

    def second_output(side):
        def body(tile):
            xs = [u4[side, tile, step] for step in range(STEPS)]
            ys = [None] * STEPS if side == 0 else [y4[0, tile, step] for step in range(STEPS)]
            ys = local_output(1, side, tile, xs, ys)
            for step in range(STEPS):
                y4[0, tile, step] = ys[step]

        return body

    loop_tiles(second_output(0))
    group_totals(1)
    loop_tiles(second_output(1))
    carries(1)

    wait_bytes(w_full.at[pl.ds(0, 2), pl.ds(0, PLANES - 1)], w_recv.at[2])
    w_half = pltpu.make_async_remote_copy(
        src_ref=w_full.at[pl.ds(2 * core, 2)],
        dst_ref=w_full.at[pl.ds(2 * core, 2)],
        send_sem=w_send.at[3],
        recv_sem=w_recv.at[3],
        device_id={"ctx": ctx + 1 - 2 * core},
        device_id_type=MESH,
    )
    w_half.start()
    wait_carries(1)

    def finish(tile):
        ys = [y4[0, tile, step] for step in range(STEPS)]
        for side in range(2):
            ys = correct(1, side, tile, ys)
        for step in range(STEPS):
            mix_f32[pl.ds(step, SUBS, stride=STEPS), :] = ys[step] * picked(p4, tile, step)
        columns = pl.ds(pl.multiple_of(tile * LANES, LANES), LANES)
        mix[tp, :, columns] = mix_f32[...].astype(BF16)
        for offset in range(1, TP):
            pltpu.make_async_remote_copy(
                src_ref=mix.at[tp, :, columns],
                dst_ref=mix.at[tp, :, columns],
                send_sem=mix_send,
                recv_sem=mix_recv.at[tp],
                device_id={"tp": lax.rem(tp + offset, TP)},
                device_id_type=MESH,
            ).start()

    loop_tiles(finish)
    w_half.wait_recv()

    def product(block):
        return lax.dot_general(
            mix[block],
            w_full[block].reshape(WIDTH, WIDTH),
            (((1,), (1,)), ((), ())),
            preferred_element_type=F32,
        )

    acc[...] = product(tp)
    for offset in range(1, TP):
        block = lax.rem(tp + offset, TP)
        wait_bytes(mix.at[block], mix_recv.at[block])
        acc[...] += product(block)
    out_ref[...] = acc[...].astype(BF16)

    for copy in par_copies:
        copy.wait_send()
    w_core.wait_send()
    w_half.wait_send()
    wait_bytes(w_planes.at[pl.ds(0, 3)], w_send.at[1])
    wait_bytes(w_full.at[pl.ds(0, 2), pl.ds(0, PLANES - 1)], w_send.at[2])
    for filt in range(2):
        wait_bytes(state_in.at[filt, pl.ds(0, GROUP - 1)], st_send.at[filt])
        wait_bytes(total_in.at[filt, pl.ds(0, PLANES - 1)], tot_send.at[filt])
        wait_bytes(carry_in.at[filt, pl.ds(0, GROUP - 1)], car_send.at[filt])
    wait_bytes(mix.at[pl.ds(0, TP - 1)], mix_send)


def local(x_gate, x_post, values, decay, residue, w_out):
    block = (POLES, LANES)
    dma = pltpu.SemaphoreType.DMA
    scratch = [
        pltpu.VMEM((CHUNK, WIDTH), BF16),
        pltpu.VMEM((CHUNK, WIDTH), BF16),
        pltpu.VMEM((CHUNK, WIDTH), BF16),
        pltpu.VMEM((2, WIDTH, POLES), F32),
        pltpu.VMEM((2, WIDTH, POLES), F32),
        pltpu.VMEM((4, TP * WIDTH), BF16),
        pltpu.VMEM((2, 2, 2, TILES) + block, F32),
        pltpu.VMEM((2, 2, TILES) + block, F32),
        pltpu.VMEM((2, 2, TILES) + block, F32),
        pltpu.VMEM((2, 2, TILES) + block, F32),
        pltpu.VMEM((TILES, CHUNK, LANES), F32),
        pltpu.VMEM((TILES, CHUNK, LANES), F32),
        pltpu.VMEM((TILES, CHUNK, LANES), F32),
        pltpu.VMEM((2, TILES, STEPS, SUBS, LANES), F32),
        pltpu.VMEM((2, TILES, STEPS, SUBS, LANES), F32),
        pltpu.VMEM((2, POLES * SUBS, LANES), F32),
        pltpu.VMEM((2, TILES, POLES * SUBS, LANES), F32),
        pltpu.VMEM((2, POLES * SUBS, LANES), F32),
        pltpu.VMEM((2, GROUP) + block, F32),
        pltpu.VMEM((2, GROUP) + block, F32),
        pltpu.VMEM((2,) + block, F32),
        pltpu.VMEM((2, PLANES) + block, F32),
        pltpu.VMEM((2, GROUP) + block, F32),
        pltpu.VMEM((2, GROUP) + block, F32),
        pltpu.VMEM((2, 4, TP * WIDTH), F32),
        pltpu.VMEM((8, TP * WIDTH), F32),
        pltpu.VMEM((4, 2, 8, WIDTH), BF16),
        pltpu.VMEM((32, WIDTH), F32),
        pltpu.VMEM((TP, PLANES, 32, WIDTH), BF16),
        pltpu.VMEM((CHUNK, LANES), F32),
        pltpu.VMEM((TP, CHUNK, WIDTH), BF16),
        pltpu.VMEM((CHUNK, WIDTH), F32),
        dma((6,)),
        dma((2,)),
        dma((2,)),
        dma((2,)),
        dma((2,)),
        dma((2,)),
        dma((2,)),
        dma((2,)),
        dma((2,)),
        dma((4,)),
        dma((4,)),
        dma,
        dma((TP,)),
    ]
    return pl.pallas_call(
        mixer_kernel,
        out_shape=jax.ShapeDtypeStruct((CHUNK, WIDTH), BF16),
        in_specs=[pl.BlockSpec(memory_space=pl.ANY)] * 6,
        out_specs=pl.BlockSpec(memory_space=pltpu.VMEM),
        scratch_shapes=scratch,
        compiler_params=pltpu.CompilerParams(
            collective_id=0, has_side_effects=True, vmem_limit_bytes=48 * 1024 * 1024
        ),
        name="mixer",
    )(x_gate, x_post, values, decay, residue, w_out)


def solution(mesh):
    in_specs = (
        P("ctx", "tp"),
        P("ctx", "tp"),
        P("ctx", "tp"),
        P(None, "tp", None),
        P(None, "tp", None),
        P(("tp", "ctx"), None),
    )
    return jax.shard_map(
        local, mesh=mesh, in_specs=in_specs, out_specs=P("ctx", "tp"), check_vma=False
    )
```

```python
import jax
import jax.numpy as jnp
from jax import lax
from jax.experimental import pallas as pl
from jax.experimental.pallas import tpu as pltpu
from jax.sharding import PartitionSpec as P

MESH = pl.DeviceIdType.MESH
F32 = jnp.float32
BF16 = jnp.bfloat16
HIGHEST = lax.Precision.HIGHEST

POLES = 16
CHUNK = 128
CHUNKS = 128
CHIPS = 64
OWN = 8
LANES = 128
TILES = 4
PLANES = 16
TP = 4
WIDTH = TILES * LANES


def far_first():
    def hops(step):
        x, y, z = (min(part, 4 - part) for part in step)
        return x + y + 4 * z

    steps = [(x, y, z) for x in range(4) for y in range(4) for z in range(4)]
    return sorted(steps[1:], key=hops, reverse=True)


STEPS = far_first()


def split(value):
    high = value.astype(BF16)
    return high, (value - high.astype(F32)).astype(BF16)


def matmul(left, right):
    return jnp.dot(left, right, preferred_element_type=F32)


def product3(left, right_high, right_low):
    high, low = split(left)
    return matmul(high, right_high) + (matmul(high, right_low) + matmul(low, right_high))


def mixer_kernel(
    gate_hbm,
    post_hbm,
    vals_hbm,
    decay_hbm,
    residue_hbm,
    w_hbm,
    out_ref,
    gate_s,
    post_s,
    vals_s,
    decay_s,
    residue_s,
    w_s,
    par_own,
    par_out,
    par_in,
    v_out,
    g_out,
    v_in,
    g_in,
    v_rows,
    g_rows,
    post_t,
    table_high,
    table_low,
    back_high,
    back_low,
    rates,
    y_rows,
    o_rows,
    y_give,
    y_take,
    y_out,
    y_in,
    w_pair,
    w_chip,
    w_planes,
    w_block,
    w_full,
    mix_f32,
    mix,
    acc,
    load_sem,
    par_send,
    par_recv,
    v_send,
    v_recv,
    g_send,
    g_recv,
    near_send,
    near_recv,
    out_send,
    out_recv,
    w_send,
    w_recv,
    mix_send,
    mix_recv,
):
    ctx = lax.axis_index("ctx")
    tp = lax.axis_index("tp")
    core = lax.rem(ctx, 2)
    chip = ctx // 2
    z_hi = lax.rem(chip, 4)
    y_pos = lax.rem(chip // 4, 4)
    x_pos = chip // 16
    plane = chip // 4
    sibling = {"ctx": ctx + 1 - 2 * core}

    def moved(step):
        x = lax.rem(x_pos + step[0], 4)
        y = lax.rem(y_pos + step[1], 4)
        z = lax.rem(z_hi + step[2], 4)
        return x * 16 + y * 4 + z

    def same_core(other_chip):
        return {"ctx": other_chip * 2 + core}

    def remote(src, dst, send_sem, recv_sem, device):
        return pltpu.make_async_remote_copy(
            src_ref=src,
            dst_ref=dst,
            send_sem=send_sem,
            recv_sem=recv_sem,
            device_id=device,
            device_id_type=MESH,
        )

    def wait_bytes(ref, sem):
        pltpu.make_async_copy(ref, ref, sem).wait()

    loads = [
        pltpu.make_async_copy(src, dst, load_sem.at[index])
        for index, (src, dst) in enumerate(
            [
                (vals_hbm, vals_s),
                (gate_hbm, gate_s),
                (decay_hbm, decay_s),
                (residue_hbm, residue_s),
                (w_hbm, w_s),
                (post_hbm, post_s),
            ]
        )
    ]
    for load in loads:
        load.start()

    barrier = pltpu.get_barrier_semaphore()
    for step in STEPS:
        pl.semaphore_signal(
            barrier, inc=1, device_id=same_core(moved(step)), device_id_type=MESH
        )
    for offset in range(1, TP):
        pl.semaphore_signal(
            barrier, inc=1, device_id={"tp": lax.rem(tp + offset, TP)}, device_id_type=MESH
        )
    pl.semaphore_signal(barrier, inc=1, device_id=sibling, device_id_type=MESH)

    def spread(source, target):
        for tile in range(TILES):
            columns = source[:, tile * LANES : (tile + 1) * LANES].astype(F32).T
            for part in range(LANES // OWN):
                target[tile * 16 + part] = columns[part * OWN : (part + 1) * OWN].astype(BF16)

    loads[0].wait()
    spread(vals_s, v_out)
    loads[1].wait()
    spread(gate_s, g_out)

    row_id = lax.broadcasted_iota(jnp.int32, (WIDTH, LANES), 0)
    own_id = lax.broadcasted_iota(jnp.int32, (WIDTH, LANES), 1) // POLES + chip * OWN
    picks = jnp.concatenate(
        [(row_id == own_id).astype(F32), (row_id == WIDTH - 1 - own_id).astype(F32)], axis=1
    )
    pole_mask = (
        lax.broadcasted_iota(jnp.int32, (2, POLES, LANES), 1)
        == lax.rem(lax.broadcasted_iota(jnp.int32, (2, POLES, LANES), 2), POLES)
    ).astype(F32)
    loads[2].wait()
    loads[3].wait()
    par_out[...] = jnp.zeros((8, LANES), F32)
    par_own[...] = jnp.zeros((8, LANES), F32)
    for which, source in enumerate((decay_s, residue_s)):
        both = lax.dot_general(
            source[...].reshape(2 * POLES, WIDTH),
            picks,
            (((1,), (0,)), ((), ())),
            precision=HIGHEST,
            preferred_element_type=F32,
        )
        for target, part in ((par_own, both[:, :LANES]), (par_out, both[:, LANES:])):
            rows = jnp.sum(part.reshape(2, POLES, LANES) * pole_mask, axis=1)
            target[2 * which : 2 * which + 2, :] = rows
    loads[4].wait()
    w_pair[core] = w_s[...].astype(F32)

    pl.semaphore_wait(barrier, len(STEPS) + (TP - 1) + 1)

    par_copy = remote(par_out, par_in, par_send, par_recv, {"tp": TP - 1 - tp})
    par_copy.start()
    for step in STEPS:
        other = moved(step)
        remote(v_out.at[other], v_in.at[chip, core], v_send, v_recv, same_core(other)).start()
    w_core = remote(w_pair.at[core], w_pair.at[core], w_send.at[0], w_recv.at[0], sibling)
    w_core.start()
    for step in STEPS:
        other = moved(step)
        remote(g_out.at[other], g_in.at[chip, core], g_send, g_recv, same_core(other)).start()
    v_in[chip, core] = v_out[chip]
    g_in[chip, core] = g_out[chip]

    w_core.wait_recv()
    w_chip[0:4, :] = w_pair[0]
    w_chip[4:8, :] = w_pair[1]
    for part in range(2):
        columns = pl.ds(pl.multiple_of((2 * core + part) * WIDTH, WIDTH), WIDTH)
        w_planes[z_hi, part] = w_chip[:, columns].astype(BF16)
    for offset in range(1, 4):
        other = plane * 4 + lax.rem(z_hi + offset, 4)
        remote(
            w_planes.at[z_hi], w_planes.at[z_hi], w_send.at[1], w_recv.at[1], same_core(other)
        ).start()

    par_copy.wait_recv()
    poles = jnp.where(core == 1, par_in[...], par_own[...])
    square = (LANES, LANES)
    row = lax.broadcasted_iota(jnp.int32, square, 0)
    col = lax.broadcasted_iota(jnp.int32, square, 1)
    row_f = row.astype(F32)
    reverse = core == 1
    tap_power = jnp.where(reverse, jnp.where(row == 0, 0.0, CHUNK - row_f), row_f)
    out_power = jnp.where(reverse, CHUNK - row_f, row_f + 1.0)
    state_power = jnp.where(reverse, row_f, CHUNK - 1.0 - row_f)
    causal = (col - row) * (1 - 2 * core) >= 0
    channel_mask = (
        lax.broadcasted_iota(jnp.int32, (OWN, LANES), 1) // POLES
        == lax.broadcasted_iota(jnp.int32, (OWN, LANES), 0)
    ).astype(F32)

    def build(filt):
        decay = poles[filt : filt + 1, :]
        weight = poles[2 + filt : 3 + filt, :] * jnp.sqrt(2.0 * decay / POLES)
        rates[filt, 0:1, :] = decay
        taps = lax.dot_general(
            channel_mask,
            weight * jnp.exp(-decay * tap_power),
            (((1,), (1,)), ((), ())),
            precision=HIGHEST,
            preferred_element_type=F32,
        )
        to_states = jnp.exp(-decay * state_power)
        from_states = (weight * jnp.exp(-decay * out_power)).T
        for channel in range(OWN):
            line = jnp.broadcast_to(taps[channel : channel + 1, :], square)
            toeplitz = pltpu.roll(line, 0, 1, stride=1, stride_axis=0)
            high, low = split(jnp.where(causal, toeplitz, 0.0))
            table_high[filt, channel, :, :LANES] = high
            table_low[filt, channel, :, :LANES] = low
            high, low = split(jnp.where(col // POLES == channel, to_states, 0.0))
            table_high[filt, channel, :, LANES:] = high
            table_low[filt, channel, :, LANES:] = low
            high, low = split(jnp.where(row // POLES == channel, from_states, 0.0))
            back_high[filt, channel] = high
            back_low[filt, channel] = low

    build(0)
    build(1)
    loads[5].wait()
    for tile in range(TILES):
        post_t[tile] = post_s[:, tile * LANES : (tile + 1) * LANES].astype(F32).T

    def gather_rows(source, target):
        def body(other, done):
            for half in range(2):
                chunk = other * 2 + half
                place = chunk + core * (CHUNKS - 1 - 2 * chunk)
                rows = pl.ds(pl.multiple_of(place * OWN, OWN), OWN)
                target[rows, :] = source[other, half].astype(F32)
            return done

        lax.fori_loop(0, CHIPS, body, 0, unroll=8)

    def picked(ref, channel):
        return ref[pl.ds(channel, CHUNKS, stride=OWN), :]

    def near(ref, index):
        return remote(
            ref.at[:, core], ref.at[:, core], near_send.at[index], near_recv.at[index], sibling
        )

    def scan(states, filt):
        decay = rates[filt, 0:1, :]

        def later(value, count):
            return jnp.where(row >= count, pltpu.roll(value, count, 0), 0.0)

        value = later(states, 1)
        for power in range(7):
            count = 2**power
            value = value + jnp.exp(-float(CHUNK * count) * decay) * later(value, count)
        return value

    wait_bytes(v_in.at[pl.ds(0, CHIPS - 1), 0], v_recv)
    v_near = near(v_in, 0)
    v_near.start()
    v_near.wait_recv()
    gather_rows(v_in, v_rows)

    states = jnp.zeros(square, F32)
    for channel in range(OWN):
        line = picked(v_rows, channel).astype(BF16)
        both = matmul(line, table_high[0, channel]) + matmul(line, table_low[0, channel])
        y_rows[channel] = both[:, :LANES]
        states = states + both[:, LANES:]
    wait_bytes(g_in.at[pl.ds(0, CHIPS - 1), 0], g_recv)
    g_near = near(g_in, 1)
    g_near.start()
    carry = scan(states, 0)
    g_near.wait_recv()
    gather_rows(g_in, g_rows)

    states = jnp.zeros(square, F32)
    for channel in range(OWN):
        value = y_rows[channel] + product3(carry, back_high[0, channel], back_low[0, channel])
        value = value * picked(g_rows, channel)
        both = product3(value, table_high[1, channel], table_low[1, channel])
        y_rows[channel] = both[:, :LANES]
        states = states + both[:, LANES:]
    carry = scan(states, 1)
    for channel in range(OWN):
        value = y_rows[channel] + product3(carry, back_high[1, channel], back_low[1, channel])
        o_rows[pl.ds(channel, CHUNKS, stride=OWN), :] = value

    for part in range(CHIPS):
        y_give[part] = o_rows[(2 * part + 1) * OWN : (2 * part + 2) * OWN, :]
    y_near = remote(y_give, y_take, near_send.at[2], near_recv.at[2], sibling)
    y_near.start()

    wait_bytes(w_planes.at[pl.ds(0, 3)], w_recv.at[1])
    for part in range(2):
        for other in range(4):
            w_block[other * 8 : other * 8 + 8, :] = w_planes[other, part].astype(F32)
        w_full[2 * core + part, plane] = w_block[...].astype(BF16)

    y_near.wait_recv()
    for part in range(CHIPS):
        place = part + core * (CHIPS - 1 - 2 * part)
        total = o_rows[2 * part * OWN : (2 * part + 1) * OWN, :] + y_take[CHIPS - 1 - part]
        y_out[place] = total.astype(BF16)
    for step in STEPS:
        other = moved(step)
        remote(
            y_out.at[other], y_in.at[chip], out_send, out_recv.at[x_pos], same_core(other)
        ).start()
    y_in[chip] = y_out[chip]
    for offset in range(1, PLANES):
        other = lax.rem(plane + offset, PLANES) * 4 + z_hi
        remote(
            w_full.at[pl.ds(2 * core, 2), plane],
            w_full.at[pl.ds(2 * core, 2), plane],
            w_send.at[2],
            w_recv.at[2],
            same_core(other),
        ).start()

    for offset in range(TILES):
        tile = lax.rem(x_pos + offset, TILES)
        wait_bytes(y_in.at[pl.ds(0, 15 if offset == 0 else 16)], out_recv.at[tile])
        for part in range(16):
            mix_f32[part * OWN : (part + 1) * OWN, :] = (
                y_in[tile * 16 + part].astype(F32)
                * post_t[tile, part * OWN : (part + 1) * OWN, :]
            )
        rows = pl.ds(pl.multiple_of(tile * LANES, LANES), LANES)
        mix[tp, rows, :] = mix_f32[...].astype(BF16)
        for other in range(1, TP):
            remote(
                mix.at[tp, rows],
                mix.at[tp, rows],
                mix_send,
                mix_recv.at[tp],
                {"tp": lax.rem(tp + other, TP)},
            ).start()

    wait_bytes(w_full.at[pl.ds(0, 2), pl.ds(0, PLANES - 1)], w_recv.at[2])
    w_half = remote(
        w_full.at[pl.ds(2 * core, 2)],
        w_full.at[pl.ds(2 * core, 2)],
        w_send.at[3],
        w_recv.at[3],
        sibling,
    )
    w_half.start()
    w_half.wait_recv()

    def project(block):
        return matmul(w_full[block].reshape(WIDTH, WIDTH), mix[block])

    acc[...] = project(tp)
    for offset in range(1, TP):
        block = lax.rem(tp + offset, TP)
        wait_bytes(mix.at[block], mix_recv.at[block])
        acc[...] += project(block)
    for tile in range(TILES):
        rows = slice(tile * LANES, (tile + 1) * LANES)
        out_ref[:, rows] = acc[rows, :].T.astype(BF16)

    par_copy.wait_send()
    wait_bytes(v_in.at[pl.ds(0, CHIPS - 1), 0], v_send)
    wait_bytes(g_in.at[pl.ds(0, CHIPS - 1), 0], g_send)
    v_near.wait_send()
    g_near.wait_send()
    y_near.wait_send()
    wait_bytes(y_in.at[pl.ds(0, CHIPS - 1)], out_send)
    w_core.wait_send()
    wait_bytes(w_planes.at[pl.ds(0, 3)], w_send.at[1])
    wait_bytes(w_full.at[pl.ds(0, 2), pl.ds(0, PLANES - 1)], w_send.at[2])
    w_half.wait_send()
    wait_bytes(mix.at[pl.ds(0, TP - 1)], mix_send)


def local(x_gate, x_post, values, decay, residue, w_out):
    dma = pltpu.SemaphoreType.DMA
    scratch = [
        pltpu.VMEM((CHUNK, WIDTH), BF16),
        pltpu.VMEM((CHUNK, WIDTH), BF16),
        pltpu.VMEM((CHUNK, WIDTH), BF16),
        pltpu.VMEM((2, POLES, WIDTH), F32),
        pltpu.VMEM((2, POLES, WIDTH), F32),
        pltpu.VMEM((4, TP * WIDTH), BF16),
        pltpu.VMEM((8, LANES), F32),
        pltpu.VMEM((8, LANES), F32),
        pltpu.VMEM((8, LANES), F32),
        pltpu.VMEM((CHIPS, OWN, CHUNK), BF16),
        pltpu.VMEM((CHIPS, OWN, CHUNK), BF16),
        pltpu.VMEM((CHIPS, 2, OWN, CHUNK), BF16),
        pltpu.VMEM((CHIPS, 2, OWN, CHUNK), BF16),
        pltpu.VMEM((CHUNKS * OWN, CHUNK), F32),
        pltpu.VMEM((CHUNKS * OWN, CHUNK), F32),
        pltpu.VMEM((TILES, LANES, CHUNK), F32),
        pltpu.VMEM((2, OWN, CHUNK, 2 * LANES), BF16),
        pltpu.VMEM((2, OWN, CHUNK, 2 * LANES), BF16),
        pltpu.VMEM((2, OWN, LANES, CHUNK), BF16),
        pltpu.VMEM((2, OWN, LANES, CHUNK), BF16),
        pltpu.VMEM((2, 8, LANES), F32),
        pltpu.VMEM((OWN, CHUNKS, CHUNK), F32),
        pltpu.VMEM((CHUNKS * OWN, CHUNK), F32),
        pltpu.VMEM((CHIPS, OWN, CHUNK), F32),
        pltpu.VMEM((CHIPS, OWN, CHUNK), F32),
        pltpu.VMEM((CHIPS, OWN, CHUNK), BF16),
        pltpu.VMEM((CHIPS, OWN, CHUNK), BF16),
        pltpu.VMEM((2, 4, TP * WIDTH), F32),
        pltpu.VMEM((8, TP * WIDTH), F32),
        pltpu.VMEM((4, 2, 8, WIDTH), BF16),
        pltpu.VMEM((32, WIDTH), F32),
        pltpu.VMEM((TP, PLANES, 32, WIDTH), BF16),
        pltpu.VMEM((LANES, CHUNK), F32),
        pltpu.VMEM((TP, WIDTH, CHUNK), BF16),
        pltpu.VMEM((WIDTH, CHUNK), F32),
        dma((6,)),
        dma,
        dma,
        dma,
        dma,
        dma,
        dma,
        dma((3,)),
        dma((3,)),
        dma,
        dma((TILES,)),
        dma((4,)),
        dma((4,)),
        dma,
        dma((TP,)),
    ]
    return pl.pallas_call(
        mixer_kernel,
        out_shape=jax.ShapeDtypeStruct((CHUNK, WIDTH), BF16),
        in_specs=[pl.BlockSpec(memory_space=pl.ANY)] * 6,
        out_specs=pl.BlockSpec(memory_space=pltpu.VMEM),
        scratch_shapes=scratch,
        compiler_params=pltpu.CompilerParams(
            collective_id=0, has_side_effects=True, vmem_limit_bytes=64 * 1024 * 1024
        ),
        name="mixer",
    )(
        x_gate,
        x_post,
        values,
        jnp.swapaxes(decay, 1, 2),
        jnp.swapaxes(residue, 1, 2),
        w_out,
    )


def solution(mesh):
    in_specs = (
        P("ctx", "tp"),
        P("ctx", "tp"),
        P("ctx", "tp"),
        P(None, "tp", None),
        P(None, "tp", None),
        P(("tp", "ctx"), None),
    )
    return jax.shard_map(
        local, mesh=mesh, in_specs=in_specs, out_specs=P("ctx", "tp"), check_vma=False
    )
```

```python
import jax
import jax.numpy as jnp
from jax import lax
from jax.experimental import pallas as pl
from jax.experimental.pallas import tpu as pltpu
from jax.sharding import PartitionSpec as P

MESH = pl.DeviceIdType.MESH
F32 = jnp.float32
BF16 = jnp.bfloat16
HIGHEST = lax.Precision.HIGHEST

POLES = 16
CHUNK = 128
CHUNKS = 128
CHIPS = 64
OWN = 8
LANES = 128
TILES = 4
PLANES = 16
TP = 4
WIDTH = TILES * LANES


def far_first():
    def hops(step):
        x, y, z = (min(part, 4 - part) for part in step)
        return x + y + 4 * z

    steps = [(x, y, z) for x in range(4) for y in range(4) for z in range(4)]
    return sorted(steps[1:], key=hops, reverse=True)


STEPS = far_first()


def split(value):
    high = value.astype(BF16)
    return high, (value - high.astype(F32)).astype(BF16)


def matmul(left, right):
    return jnp.dot(left, right, preferred_element_type=F32)


def product3(left, right_high, right_low):
    high, low = split(left)
    return matmul(high, right_high) + (matmul(high, right_low) + matmul(low, right_high))


def mixer_kernel(
    gate_hbm,
    post_hbm,
    vals_hbm,
    decay_hbm,
    residue_hbm,
    w_hbm,
    out_ref,
    gate_s,
    post_s,
    vals_s,
    decay_s,
    residue_s,
    w_s,
    par_own,
    par_out,
    par_in,
    vg_out,
    vg_in,
    v_rows,
    g_rows,
    post_t,
    table_high,
    table_low,
    back_high,
    back_low,
    rates,
    y_rows,
    o_rows,
    y_give,
    y_take,
    y_out,
    y_in,
    w_pair,
    w_chip,
    w_planes,
    w_block,
    w_full,
    mix_f32,
    mix,
    acc,
    load_sem,
    par_send,
    par_recv,
    vg_send,
    vg_recv,
    near_send,
    near_recv,
    out_send,
    out_recv,
    w_send,
    w_recv,
    mix_send,
    mix_recv,
):
    ctx = lax.axis_index("ctx")
    tp = lax.axis_index("tp")
    core = lax.rem(ctx, 2)
    chip = ctx // 2
    z_hi = lax.rem(chip, 4)
    y_pos = lax.rem(chip // 4, 4)
    x_pos = chip // 16
    plane = chip // 4
    sibling = {"ctx": ctx + 1 - 2 * core}
    tp_peers = (tp + 1 - 2 * lax.rem(tp, 2), lax.rem(tp + 2, TP), TP - 1 - tp)

    def moved(step):
        x = lax.rem(x_pos + step[0], 4)
        y = lax.rem(y_pos + step[1], 4)
        z = lax.rem(z_hi + step[2], 4)
        return x * 16 + y * 4 + z

    def same_core(other_chip):
        return {"ctx": other_chip * 2 + core}

    def remote(src, dst, send_sem, recv_sem, device):
        return pltpu.make_async_remote_copy(
            src_ref=src,
            dst_ref=dst,
            send_sem=send_sem,
            recv_sem=recv_sem,
            device_id=device,
            device_id_type=MESH,
        )

    def wait_bytes(ref, sem):
        pltpu.make_async_copy(ref, ref, sem).wait()

    loads = [
        pltpu.make_async_copy(src, dst, load_sem.at[index])
        for index, (src, dst) in enumerate(
            [
                (vals_hbm, vals_s),
                (gate_hbm, gate_s),
                (decay_hbm, decay_s),
                (residue_hbm, residue_s),
                (w_hbm, w_s),
                (post_hbm, post_s),
            ]
        )
    ]
    for load in loads:
        load.start()

    barrier = pltpu.get_barrier_semaphore()
    for step in STEPS:
        pl.semaphore_signal(
            barrier, inc=1, device_id=same_core(moved(step)), device_id_type=MESH
        )
    for other in tp_peers:
        pl.semaphore_signal(barrier, inc=1, device_id={"tp": other}, device_id_type=MESH)
    pl.semaphore_signal(barrier, inc=1, device_id=sibling, device_id_type=MESH)

    for which, source in enumerate((vals_s, gate_s)):
        loads[which].wait()
        for tile in range(TILES):
            columns = source[:, tile * LANES : (tile + 1) * LANES].astype(F32).T
            for part in range(LANES // OWN):
                piece = columns[part * OWN : (part + 1) * OWN]
                vg_out[tile * 16 + part, which] = piece.astype(BF16)

    row_id = lax.broadcasted_iota(jnp.int32, (WIDTH, LANES), 0)
    own_id = lax.broadcasted_iota(jnp.int32, (WIDTH, LANES), 1) // POLES + chip * OWN
    picks = jnp.concatenate(
        [(row_id == own_id).astype(F32), (row_id == WIDTH - 1 - own_id).astype(F32)], axis=1
    )
    pole_mask = (
        lax.broadcasted_iota(jnp.int32, (2, POLES, LANES), 1)
        == lax.rem(lax.broadcasted_iota(jnp.int32, (2, POLES, LANES), 2), POLES)
    ).astype(F32)
    loads[2].wait()
    loads[3].wait()
    par_out[...] = jnp.zeros((8, LANES), F32)
    par_own[...] = jnp.zeros((8, LANES), F32)
    for which, source in enumerate((decay_s, residue_s)):
        both = lax.dot_general(
            source[...].reshape(2 * POLES, WIDTH),
            picks,
            (((1,), (0,)), ((), ())),
            precision=HIGHEST,
            preferred_element_type=F32,
        )
        for target, part in ((par_own, both[:, :LANES]), (par_out, both[:, LANES:])):
            rows = jnp.sum(part.reshape(2, POLES, LANES) * pole_mask, axis=1)
            target[2 * which : 2 * which + 2, :] = rows
    loads[4].wait()
    w_pair[core] = w_s[...].astype(F32)

    pl.semaphore_wait(barrier, len(STEPS) + (TP - 1) + 1)

    par_copy = remote(par_out, par_in, par_send, par_recv, {"tp": TP - 1 - tp})
    par_copy.start()
    w_core = remote(w_pair.at[core], w_pair.at[core], w_send.at[0], w_recv.at[0], sibling)
    w_core.start()
    for step in STEPS:
        other = moved(step)
        remote(vg_out.at[other], vg_in.at[chip, core], vg_send, vg_recv, same_core(other)).start()
    vg_in[chip, core] = vg_out[chip]

    w_core.wait_recv()
    w_chip[0:4, :] = w_pair[0]
    w_chip[4:8, :] = w_pair[1]
    for part in range(2):
        columns = pl.ds(pl.multiple_of((2 * core + part) * WIDTH, WIDTH), WIDTH)
        w_planes[z_hi, part] = w_chip[:, columns].astype(BF16)
    for offset in range(1, 4):
        other = plane * 4 + lax.rem(z_hi + offset, 4)
        remote(
            w_planes.at[z_hi], w_planes.at[z_hi], w_send.at[1], w_recv.at[1], same_core(other)
        ).start()

    par_copy.wait_recv()
    poles = jnp.where(core == 1, par_in[...], par_own[...])
    square = (LANES, LANES)
    row = lax.broadcasted_iota(jnp.int32, square, 0)
    col = lax.broadcasted_iota(jnp.int32, square, 1)
    row_f = row.astype(F32)
    reverse = core == 1
    tap_power = jnp.where(reverse, jnp.where(row == 0, 0.0, CHUNK - row_f), row_f)
    out_power = jnp.where(reverse, CHUNK - row_f, row_f + 1.0)
    state_power = jnp.where(reverse, row_f, CHUNK - 1.0 - row_f)
    causal = (col - row) * (1 - 2 * core) >= 0
    channel_mask = (
        lax.broadcasted_iota(jnp.int32, (OWN, LANES), 1) // POLES
        == lax.broadcasted_iota(jnp.int32, (OWN, LANES), 0)
    ).astype(F32)

    def build(filt):
        decay = poles[filt : filt + 1, :]
        weight = poles[2 + filt : 3 + filt, :] * jnp.sqrt(2.0 * decay / POLES)
        rates[filt, 0:1, :] = decay
        taps = lax.dot_general(
            channel_mask,
            weight * jnp.exp(-decay * tap_power),
            (((1,), (1,)), ((), ())),
            precision=HIGHEST,
            preferred_element_type=F32,
        )
        to_states = jnp.exp(-decay * state_power)
        from_states = (weight * jnp.exp(-decay * out_power)).T
        for channel in range(OWN):
            line = jnp.broadcast_to(taps[channel : channel + 1, :], square)
            toeplitz = pltpu.roll(line, 0, 1, stride=1, stride_axis=0)
            high, low = split(jnp.where(causal, toeplitz, 0.0))
            table_high[filt, channel, :, :LANES] = high
            table_low[filt, channel, :, :LANES] = low
            high, low = split(jnp.where(col // POLES == channel, to_states, 0.0))
            table_high[filt, channel, :, LANES:] = high
            table_low[filt, channel, :, LANES:] = low
            high, low = split(jnp.where(row // POLES == channel, from_states, 0.0))
            back_high[filt, channel] = high
            back_low[filt, channel] = low

    build(0)
    build(1)
    loads[5].wait()
    for tile in range(TILES):
        post_t[tile] = post_s[:, tile * LANES : (tile + 1) * LANES].astype(F32).T

    def gather_rows(which, target):
        def body(other, done):
            for half in range(2):
                chunk = other * 2 + half
                place = chunk + core * (CHUNKS - 1 - 2 * chunk)
                rows = pl.ds(pl.multiple_of(place * OWN, OWN), OWN)
                target[rows, :] = vg_in[other, half, which].astype(F32)
            return done

        lax.fori_loop(0, CHIPS, body, 0, unroll=8)

    def picked(ref, channel):
        return ref[pl.ds(channel, CHUNKS, stride=OWN), :]

    def near(which):
        part = vg_in.at[:, core, which]
        return remote(part, part, near_send.at[which], near_recv.at[which], sibling)

    def scan(states, filt):
        decay = rates[filt, 0:1, :]

        def later(value, count):
            return jnp.where(row >= count, pltpu.roll(value, count, 0), 0.0)

        value = later(states, 1)
        for power in range(7):
            count = 2**power
            value = value + jnp.exp(-float(CHUNK * count) * decay) * later(value, count)
        return value

    wait_bytes(vg_in.at[pl.ds(0, CHIPS - 1), 0], vg_recv)
    v_near = near(0)
    v_near.start()
    g_near = near(1)
    g_near.start()

    wait_bytes(w_planes.at[pl.ds(0, 3)], w_recv.at[1])
    for part in range(2):
        for other in range(4):
            w_block[other * 8 : other * 8 + 8, :] = w_planes[other, part].astype(F32)
        w_full[2 * core + part, plane] = w_block[...].astype(BF16)
    for offset in range(1, PLANES):
        other = lax.rem(plane + offset, PLANES) * 4 + z_hi
        remote(
            w_full.at[pl.ds(2 * core, 2), plane],
            w_full.at[pl.ds(2 * core, 2), plane],
            w_send.at[2],
            w_recv.at[2],
            same_core(other),
        ).start()

    v_near.wait_recv()
    gather_rows(0, v_rows)

    states = jnp.zeros(square, F32)
    for channel in range(OWN):
        line = picked(v_rows, channel).astype(BF16)
        both = matmul(line, table_high[0, channel]) + matmul(line, table_low[0, channel])
        y_rows[channel] = both[:, :LANES]
        states = states + both[:, LANES:]
    carry = scan(states, 0)
    g_near.wait_recv()
    gather_rows(1, g_rows)

    states = jnp.zeros(square, F32)
    for channel in range(OWN):
        value = y_rows[channel] + product3(carry, back_high[0, channel], back_low[0, channel])
        value = value * picked(g_rows, channel)
        both = product3(value, table_high[1, channel], table_low[1, channel])
        y_rows[channel] = both[:, :LANES]
        states = states + both[:, LANES:]
    carry = scan(states, 1)
    for channel in range(OWN):
        value = y_rows[channel] + product3(carry, back_high[1, channel], back_low[1, channel])
        o_rows[pl.ds(channel, CHUNKS, stride=OWN), :] = value

    for part in range(CHIPS):
        y_give[part] = o_rows[(2 * part + 1) * OWN : (2 * part + 2) * OWN, :]
    y_near = remote(y_give, y_take, near_send.at[2], near_recv.at[2], sibling)
    y_near.start()

    y_near.wait_recv()
    for part in range(CHIPS):
        place = part + core * (CHIPS - 1 - 2 * part)
        total = o_rows[2 * part * OWN : (2 * part + 1) * OWN, :] + y_take[CHIPS - 1 - part]
        y_out[place] = total.astype(BF16)
    for step in STEPS:
        other = moved(step)
        remote(
            y_out.at[other], y_in.at[chip], out_send, out_recv.at[x_pos], same_core(other)
        ).start()
    y_in[chip] = y_out[chip]

    wait_bytes(w_full.at[pl.ds(0, 2), pl.ds(0, PLANES - 1)], w_recv.at[2])
    w_half = remote(
        w_full.at[pl.ds(2 * core, 2)],
        w_full.at[pl.ds(2 * core, 2)],
        w_send.at[3],
        w_recv.at[3],
        sibling,
    )
    w_half.start()

    for offset in range(TILES):
        tile = lax.rem(x_pos + offset, TILES)
        wait_bytes(y_in.at[pl.ds(0, 15 if offset == 0 else 16)], out_recv.at[tile])
        for part in range(16):
            mix_f32[part * OWN : (part + 1) * OWN, :] = (
                y_in[tile * 16 + part].astype(F32)
                * post_t[tile, part * OWN : (part + 1) * OWN, :]
            )
        rows = pl.ds(pl.multiple_of(tile * LANES, LANES), LANES)
        mix[tp, rows, :] = mix_f32[...].astype(BF16)
        for other in reversed(tp_peers):
            remote(
                mix.at[tp, rows], mix.at[tp, rows], mix_send, mix_recv.at[tp], {"tp": other}
            ).start()

    w_half.wait_recv()

    def project(block):
        return matmul(w_full[block].reshape(WIDTH, WIDTH), mix[block])

    acc[...] = project(tp)
    for block in tp_peers:
        wait_bytes(mix.at[block], mix_recv.at[block])
        acc[...] += project(block)
    for tile in range(TILES):
        rows = slice(tile * LANES, (tile + 1) * LANES)
        out_ref[:, rows] = acc[rows, :].T.astype(BF16)

    par_copy.wait_send()
    wait_bytes(vg_in.at[pl.ds(0, CHIPS - 1), 0], vg_send)
    v_near.wait_send()
    g_near.wait_send()
    y_near.wait_send()
    wait_bytes(y_in.at[pl.ds(0, CHIPS - 1)], out_send)
    w_core.wait_send()
    wait_bytes(w_planes.at[pl.ds(0, 3)], w_send.at[1])
    wait_bytes(w_full.at[pl.ds(0, 2), pl.ds(0, PLANES - 1)], w_send.at[2])
    w_half.wait_send()
    wait_bytes(mix.at[pl.ds(0, TP - 1)], mix_send)


def local(x_gate, x_post, values, decay, residue, w_out):
    dma = pltpu.SemaphoreType.DMA
    scratch = [
        pltpu.VMEM((CHUNK, WIDTH), BF16),
        pltpu.VMEM((CHUNK, WIDTH), BF16),
        pltpu.VMEM((CHUNK, WIDTH), BF16),
        pltpu.VMEM((2, POLES, WIDTH), F32),
        pltpu.VMEM((2, POLES, WIDTH), F32),
        pltpu.VMEM((4, TP * WIDTH), BF16),
        pltpu.VMEM((8, LANES), F32),
        pltpu.VMEM((8, LANES), F32),
        pltpu.VMEM((8, LANES), F32),
        pltpu.VMEM((CHIPS, 2, OWN, CHUNK), BF16),
        pltpu.VMEM((CHIPS, 2, 2, OWN, CHUNK), BF16),
        pltpu.VMEM((CHUNKS * OWN, CHUNK), F32),
        pltpu.VMEM((CHUNKS * OWN, CHUNK), F32),
        pltpu.VMEM((TILES, LANES, CHUNK), F32),
        pltpu.VMEM((2, OWN, CHUNK, 2 * LANES), BF16),
        pltpu.VMEM((2, OWN, CHUNK, 2 * LANES), BF16),
        pltpu.VMEM((2, OWN, LANES, CHUNK), BF16),
        pltpu.VMEM((2, OWN, LANES, CHUNK), BF16),
        pltpu.VMEM((2, 8, LANES), F32),
        pltpu.VMEM((OWN, CHUNKS, CHUNK), F32),
        pltpu.VMEM((CHUNKS * OWN, CHUNK), F32),
        pltpu.VMEM((CHIPS, OWN, CHUNK), F32),
        pltpu.VMEM((CHIPS, OWN, CHUNK), F32),
        pltpu.VMEM((CHIPS, OWN, CHUNK), BF16),
        pltpu.VMEM((CHIPS, OWN, CHUNK), BF16),
        pltpu.VMEM((2, 4, TP * WIDTH), F32),
        pltpu.VMEM((8, TP * WIDTH), F32),
        pltpu.VMEM((4, 2, 8, WIDTH), BF16),
        pltpu.VMEM((32, WIDTH), F32),
        pltpu.VMEM((TP, PLANES, 32, WIDTH), BF16),
        pltpu.VMEM((LANES, CHUNK), F32),
        pltpu.VMEM((TP, WIDTH, CHUNK), BF16),
        pltpu.VMEM((WIDTH, CHUNK), F32),
        dma((6,)),
        dma,
        dma,
        dma,
        dma,
        dma((3,)),
        dma((3,)),
        dma,
        dma((TILES,)),
        dma((4,)),
        dma((4,)),
        dma,
        dma((TP,)),
    ]
    return pl.pallas_call(
        mixer_kernel,
        out_shape=jax.ShapeDtypeStruct((CHUNK, WIDTH), BF16),
        in_specs=[pl.BlockSpec(memory_space=pl.ANY)] * 6,
        out_specs=pl.BlockSpec(memory_space=pltpu.VMEM),
        scratch_shapes=scratch,
        compiler_params=pltpu.CompilerParams(
            collective_id=0, has_side_effects=True, vmem_limit_bytes=48 * 1024 * 1024
        ),
        name="mixer",
    )(
        *(
            pltpu.with_memory_space_constraint(array, pltpu.HBM)
            for array in (
                x_gate,
                x_post,
                values,
                jnp.swapaxes(decay, 1, 2),
                jnp.swapaxes(residue, 1, 2),
                w_out,
            )
        )
    )


def solution(mesh):
    in_specs = (
        P("ctx", "tp"),
        P("ctx", "tp"),
        P("ctx", "tp"),
        P(None, "tp", None),
        P(None, "tp", None),
        P(("tp", "ctx"), None),
    )
    return jax.shard_map(
        local, mesh=mesh, in_specs=in_specs, out_specs=P("ctx", "tp"), check_vma=False
    )
```

```python
import jax
import jax.numpy as jnp
from jax import lax
from jax.experimental import pallas as pl
from jax.experimental.pallas import tpu as pltpu
from jax.sharding import PartitionSpec as P

MESH = pl.DeviceIdType.MESH
F32 = jnp.float32
BF16 = jnp.bfloat16
HIGHEST = lax.Precision.HIGHEST

POLES = 16
CHUNK = 128
CHUNKS = 128
CHIPS = 64
OWN = 8
LANES = 128
TILES = 4
PLANES = 16
TP = 4
WIDTH = TILES * LANES


def far_first():
    def hops(step):
        x, y, z = (min(part, 4 - part) for part in step)
        return x + y + 4 * z

    steps = [(x, y, z) for x in range(4) for y in range(4) for z in range(4)]
    return sorted(steps[1:], key=hops, reverse=True)


STEPS = far_first()
PLANE_OFFSETS = [step[:2] for step in STEPS if step[2] == 0]


def split(value):
    high = value.astype(BF16)
    return high, (value - high.astype(F32)).astype(BF16)


def matmul(left, right):
    return jnp.dot(left, right, preferred_element_type=F32)


def product3(left, right_high, right_low):
    high, low = split(left)
    return matmul(high, right_high) + (matmul(high, right_low) + matmul(low, right_high))


def mixer_kernel(
    gate_hbm,
    post_hbm,
    vals_hbm,
    decay_hbm,
    residue_hbm,
    w_hbm,
    out_ref,
    gate_s,
    post_s,
    vals_s,
    decay_s,
    residue_s,
    w_s,
    par_own,
    par_out,
    par_in,
    v_out,
    g_out,
    v_in,
    g_in,
    v_rows,
    g_rows,
    post_t,
    table_high,
    table_low,
    back_high,
    back_low,
    rates,
    y_rows,
    o_rows,
    y_give,
    y_take,
    y_out,
    y_in,
    w_planes,
    w_block,
    w_full,
    mix_f32,
    mix,
    acc,
    sums,
    load_sem,
    par_send,
    par_recv,
    v_send,
    v_recv,
    g_send,
    g_recv,
    near_send,
    near_recv,
    out_send,
    out_recv,
    w_send,
    w_recv,
    mix_send,
    mix_recv,
):
    ctx = lax.axis_index("ctx")
    tp = lax.axis_index("tp")
    core = lax.rem(ctx, 2)
    chip = ctx // 2
    z_hi = lax.rem(chip, 4)
    y_pos = lax.rem(chip // 4, 4)
    x_pos = chip // 16
    plane = chip // 4
    sibling = {"ctx": ctx + 1 - 2 * core}
    tp_peers = (tp + 1 - 2 * lax.rem(tp, 2), lax.rem(tp + 2, TP), TP - 1 - tp)

    def moved(step):
        x = lax.rem(x_pos + step[0], 4)
        y = lax.rem(y_pos + step[1], 4)
        z = lax.rem(z_hi + step[2], 4)
        return x * 16 + y * 4 + z

    def same_core(other_chip):
        return {"ctx": other_chip * 2 + core}

    def remote(src, dst, send_sem, recv_sem, device):
        return pltpu.make_async_remote_copy(
            src_ref=src,
            dst_ref=dst,
            send_sem=send_sem,
            recv_sem=recv_sem,
            device_id=device,
            device_id_type=MESH,
        )

    def wait_bytes(ref, sem):
        pltpu.make_async_copy(ref, ref, sem).wait()

    loads = [
        pltpu.make_async_copy(src, dst, load_sem.at[index])
        for index, (src, dst) in enumerate(
            [
                (vals_hbm, vals_s),
                (gate_hbm, gate_s),
                (decay_hbm, decay_s),
                (residue_hbm, residue_s),
                (w_hbm, w_s),
                (post_hbm, post_s),
            ]
        )
    ]
    for load in loads:
        load.start()

    barrier = pltpu.get_barrier_semaphore()
    for step in STEPS:
        pl.semaphore_signal(
            barrier, inc=1, device_id=same_core(moved(step)), device_id_type=MESH
        )
    for other in tp_peers:
        pl.semaphore_signal(barrier, inc=1, device_id={"tp": other}, device_id_type=MESH)
    pl.semaphore_signal(barrier, inc=1, device_id=sibling, device_id_type=MESH)

    def spread(source, target):
        for tile in range(TILES):
            columns = source[:, tile * LANES : (tile + 1) * LANES].astype(F32).T
            for part in range(LANES // OWN):
                target[tile * 16 + part] = columns[part * OWN : (part + 1) * OWN].astype(BF16)

    loads[0].wait()
    spread(vals_s, v_out)
    loads[1].wait()
    spread(gate_s, g_out)

    row_id = lax.broadcasted_iota(jnp.int32, (WIDTH, LANES), 0)
    own_id = lax.broadcasted_iota(jnp.int32, (WIDTH, LANES), 1) // POLES + chip * OWN
    picks = jnp.concatenate(
        [(row_id == own_id).astype(F32), (row_id == WIDTH - 1 - own_id).astype(F32)], axis=1
    )
    pole_mask = (
        lax.broadcasted_iota(jnp.int32, (2, POLES, LANES), 1)
        == lax.rem(lax.broadcasted_iota(jnp.int32, (2, POLES, LANES), 2), POLES)
    ).astype(F32)
    loads[2].wait()
    loads[3].wait()
    par_out[...] = jnp.zeros((8, LANES), F32)
    par_own[...] = jnp.zeros((8, LANES), F32)
    for which, source in enumerate((decay_s, residue_s)):
        both = lax.dot_general(
            source[...].reshape(2 * POLES, WIDTH),
            picks,
            (((1,), (0,)), ((), ())),
            precision=HIGHEST,
            preferred_element_type=F32,
        )
        for target, part in ((par_own, both[:, :LANES]), (par_out, both[:, LANES:])):
            rows = jnp.sum(part.reshape(2, POLES, LANES) * pole_mask, axis=1)
            target[2 * which : 2 * which + 2, :] = rows
    loads[4].wait()
    w_planes[z_hi] = w_s[...]

    pl.semaphore_wait(barrier, len(STEPS) + (TP - 1) + 1)

    par_copy = remote(par_out, par_in, par_send, par_recv, {"tp": TP - 1 - tp})
    par_copy.start()
    for step in STEPS:
        other = moved(step)
        remote(v_out.at[other], v_in.at[chip, core], v_send, v_recv, same_core(other)).start()
    v_in[chip, core] = v_out[chip]

    for offset in (2, 1, 3):
        other = plane * 4 + lax.rem(z_hi + offset, 4)
        remote(
            w_planes.at[z_hi], w_planes.at[z_hi], w_send.at[0], w_recv.at[0], same_core(other)
        ).start()
    for step in STEPS:
        other = moved(step)
        remote(g_out.at[other], g_in.at[chip, core], g_send, g_recv, same_core(other)).start()
    g_in[chip, core] = g_out[chip]

    par_copy.wait_recv()
    poles = jnp.where(core == 1, par_in[...], par_own[...])
    square = (LANES, LANES)
    row = lax.broadcasted_iota(jnp.int32, square, 0)
    col = lax.broadcasted_iota(jnp.int32, square, 1)
    row_f = row.astype(F32)
    reverse = core == 1
    tap_power = jnp.where(reverse, jnp.where(row == 0, 0.0, CHUNK - row_f), row_f)
    out_power = jnp.where(reverse, CHUNK - row_f, row_f + 1.0)
    state_power = jnp.where(reverse, row_f, CHUNK - 1.0 - row_f)
    causal = (col - row) * (1 - 2 * core) >= 0
    channel_mask = (
        lax.broadcasted_iota(jnp.int32, (OWN, LANES), 1) // POLES
        == lax.broadcasted_iota(jnp.int32, (OWN, LANES), 0)
    ).astype(F32)

    def build(filt):
        decay = poles[filt : filt + 1, :]
        weight = poles[2 + filt : 3 + filt, :] * jnp.sqrt(2.0 * decay / POLES)
        rates[filt, 0:1, :] = decay
        taps = lax.dot_general(
            channel_mask,
            weight * jnp.exp(-decay * tap_power),
            (((1,), (1,)), ((), ())),
            precision=HIGHEST,
            preferred_element_type=F32,
        )
        to_states = jnp.exp(-decay * state_power)
        from_states = (weight * jnp.exp(-decay * out_power)).T
        for channel in range(OWN):
            line = jnp.broadcast_to(taps[channel : channel + 1, :], square)
            toeplitz = pltpu.roll(line, 0, 1, stride=1, stride_axis=0)
            high, low = split(jnp.where(causal, toeplitz, 0.0))
            table_high[filt, channel, :, :LANES] = high
            table_low[filt, channel, :, :LANES] = low
            high, low = split(jnp.where(col // POLES == channel, to_states, 0.0))
            table_high[filt, channel, :, LANES:] = high
            table_low[filt, channel, :, LANES:] = low
            high, low = split(jnp.where(row // POLES == channel, from_states, 0.0))
            back_high[filt, channel] = high
            back_low[filt, channel] = low

    build(0)
    build(1)
    loads[5].wait()
    for tile in range(TILES):
        post_t[tile] = post_s[:, tile * LANES : (tile + 1) * LANES].astype(F32).T

    def gather_rows(source, target):
        def body(other, done):
            for half in range(2):
                chunk = other * 2 + half
                place = chunk + core * (CHUNKS - 1 - 2 * chunk)
                rows = pl.ds(pl.multiple_of(place * OWN, OWN), OWN)
                target[rows, :] = source[other, half].astype(F32)
            return done

        lax.fori_loop(0, CHIPS, body, 0, unroll=8)

    def picked(ref, channel):
        return ref[pl.ds(channel, CHUNKS, stride=OWN), :]

    def near(ref, index):
        part = ref.at[:, core]
        return remote(part, part, near_send.at[index], near_recv.at[index], sibling)

    def scan(states, filt):
        decay = rates[filt, 0:1, :]

        def later(value, count):
            return jnp.where(row >= count, pltpu.roll(value, count, 0), 0.0)

        value = later(states, 1)
        for power in range(7):
            count = 2**power
            value = value + jnp.exp(-float(CHUNK * count) * decay) * later(value, count)
        return value

    wait_bytes(w_planes.at[pl.ds(0, 3)], w_recv.at[0])
    for other in range(4):
        w_block[other * 4 : other * 4 + 4, :] = w_planes[other].astype(F32)
    for block in range(TP):
        columns = slice(block * WIDTH, (block + 1) * WIDTH)
        w_full[block, core, plane] = w_block[:, columns].astype(BF16)
    for offset in PLANE_OFFSETS:
        x = lax.rem(x_pos + offset[0], 4)
        y = lax.rem(y_pos + offset[1], 4)
        part = w_full.at[:, core, plane]
        remote(
            part, part, w_send.at[1], w_recv.at[1], same_core(x * 16 + y * 4 + z_hi)
        ).start()

    wait_bytes(v_in.at[pl.ds(0, CHIPS - 1), 0], v_recv)
    v_near = near(v_in, 0)
    v_near.start()
    v_near.wait_recv()
    gather_rows(v_in, v_rows)

    states = jnp.zeros(square, F32)
    for channel in range(OWN):
        line = picked(v_rows, channel).astype(BF16)
        both = matmul(line, table_high[0, channel]) + matmul(line, table_low[0, channel])
        y_rows[channel] = both[:, :LANES]
        states = states + both[:, LANES:]
    carry = scan(states, 0)
    wait_bytes(g_in.at[pl.ds(0, CHIPS - 1), 0], g_recv)
    g_near = near(g_in, 1)
    g_near.start()
    g_near.wait_recv()
    gather_rows(g_in, g_rows)

    states = jnp.zeros(square, F32)
    for channel in range(OWN):
        value = y_rows[channel] + product3(carry, back_high[0, channel], back_low[0, channel])
        value = value * picked(g_rows, channel)
        both = product3(value, table_high[1, channel], table_low[1, channel])
        y_rows[channel] = both[:, :LANES]
        states = states + both[:, LANES:]
    carry = scan(states, 1)

    y_near = []
    for half in range(2):
        chunks = slice(half * CHIPS, (half + 1) * CHIPS)
        parts = range(half * CHIPS // 2, (half + 1) * CHIPS // 2)
        high, low = split(carry[chunks])
        for channel in range(OWN):
            value = y_rows[channel, chunks, :] + (
                matmul(high, back_high[1, channel])
                + (matmul(high, back_low[1, channel]) + matmul(low, back_high[1, channel]))
            )
            o_rows[pl.ds(half * CHIPS * OWN + channel, CHIPS, stride=OWN), :] = value
        for part in parts:
            y_give[part] = o_rows[(2 * part + 1) * OWN : (2 * part + 2) * OWN, :]
        piece = pl.ds(half * CHIPS // 2, CHIPS // 2)
        copy = remote(
            y_give.at[piece],
            y_take.at[piece],
            near_send.at[2 + half],
            near_recv.at[2 + half],
            sibling,
        )
        copy.start()
        y_near.append(copy)
    for half in (1, 0):
        y_near[1 - half].wait_recv()
        for part in range(half * CHIPS // 2, (half + 1) * CHIPS // 2):
            place = part + core * (CHIPS - 1 - 2 * part)
            total = o_rows[2 * part * OWN : (2 * part + 1) * OWN, :] + y_take[CHIPS - 1 - part]
            y_out[place] = total.astype(BF16)
    for step in STEPS:
        other = moved(step)
        remote(
            y_out.at[other], y_in.at[chip], out_send, out_recv.at[x_pos], same_core(other)
        ).start()
    y_in[chip] = y_out[chip]

    wait_bytes(w_full.at[:, 0, pl.ds(0, PLANES - 1)], w_recv.at[1])
    part = w_full.at[:, core]
    w_half = remote(part, part, w_send.at[2], w_recv.at[2], sibling)
    w_half.start()

    for offset in range(TILES):
        tile = lax.rem(x_pos + offset, TILES)
        wait_bytes(y_in.at[pl.ds(0, 15 if offset == 0 else 16)], out_recv.at[tile])
        for part in range(16):
            mix_f32[part * OWN : (part + 1) * OWN, :] = (
                y_in[tile * 16 + part].astype(F32)
                * post_t[tile, part * OWN : (part + 1) * OWN, :]
            )
        rows = pl.ds(pl.multiple_of(tile * LANES, LANES), LANES)
        mix[tp, rows, :] = mix_f32[...].astype(BF16)
        for other in reversed(tp_peers):
            remote(
                mix.at[tp, rows], mix.at[tp, rows], mix_send, mix_recv.at[tp], {"tp": other}
            ).start()

    w_half.wait_recv()

    def project(block):
        return matmul(w_full[block].reshape(WIDTH, WIDTH), mix[block])

    acc[...] = project(tp)
    for block in tp_peers:
        wait_bytes(mix.at[block], mix_recv.at[block])
        acc[...] += project(block)
    for group in range(CHIPS):
        for part in range(2):
            first = part * (WIDTH // 2) + group * 4
            sums[group * 8 + part * 4 : group * 8 + part * 4 + 4, :] = acc[first : first + 4, :]
    for tile in range(TILES):
        rows = slice(tile * LANES, (tile + 1) * LANES)
        out_ref[:, rows] = sums[rows, :].T.astype(BF16)

    par_copy.wait_send()
    wait_bytes(v_in.at[pl.ds(0, CHIPS - 1), 0], v_send)
    wait_bytes(g_in.at[pl.ds(0, CHIPS - 1), 0], g_send)
    v_near.wait_send()
    g_near.wait_send()
    for copy in y_near:
        copy.wait_send()
    wait_bytes(y_in.at[pl.ds(0, CHIPS - 1)], out_send)
    wait_bytes(w_planes.at[pl.ds(0, 3)], w_send.at[0])
    wait_bytes(w_full.at[:, 0, pl.ds(0, PLANES - 1)], w_send.at[1])
    w_half.wait_send()
    wait_bytes(mix.at[pl.ds(0, TP - 1)], mix_send)


def local(x_gate, x_post, values, decay, residue, w_out):
    dma = pltpu.SemaphoreType.DMA
    scratch = [
        pltpu.VMEM((CHUNK, WIDTH), BF16),
        pltpu.VMEM((CHUNK, WIDTH), BF16),
        pltpu.VMEM((CHUNK, WIDTH), BF16),
        pltpu.VMEM((2, POLES, WIDTH), F32),
        pltpu.VMEM((2, POLES, WIDTH), F32),
        pltpu.VMEM((4, TP * WIDTH), BF16),
        pltpu.VMEM((8, LANES), F32),
        pltpu.VMEM((8, LANES), F32),
        pltpu.VMEM((8, LANES), F32),
        pltpu.VMEM((CHIPS, OWN, CHUNK), BF16),
        pltpu.VMEM((CHIPS, OWN, CHUNK), BF16),
        pltpu.VMEM((CHIPS, 2, OWN, CHUNK), BF16),
        pltpu.VMEM((CHIPS, 2, OWN, CHUNK), BF16),
        pltpu.VMEM((CHUNKS * OWN, CHUNK), F32),
        pltpu.VMEM((CHUNKS * OWN, CHUNK), F32),
        pltpu.VMEM((TILES, LANES, CHUNK), F32),
        pltpu.VMEM((2, OWN, CHUNK, 2 * LANES), BF16),
        pltpu.VMEM((2, OWN, CHUNK, 2 * LANES), BF16),
        pltpu.VMEM((2, OWN, LANES, CHUNK), BF16),
        pltpu.VMEM((2, OWN, LANES, CHUNK), BF16),
        pltpu.VMEM((2, 8, LANES), F32),
        pltpu.VMEM((OWN, CHUNKS, CHUNK), F32),
        pltpu.VMEM((CHUNKS * OWN, CHUNK), F32),
        pltpu.VMEM((CHIPS, OWN, CHUNK), F32),
        pltpu.VMEM((CHIPS, OWN, CHUNK), F32),
        pltpu.VMEM((CHIPS, OWN, CHUNK), BF16),
        pltpu.VMEM((CHIPS, OWN, CHUNK), BF16),
        pltpu.VMEM((4, 4, TP * WIDTH), BF16),
        pltpu.VMEM((16, TP * WIDTH), F32),
        pltpu.VMEM((TP, 2, PLANES, 16, WIDTH), BF16),
        pltpu.VMEM((LANES, CHUNK), F32),
        pltpu.VMEM((TP, WIDTH, CHUNK), BF16),
        pltpu.VMEM((WIDTH, CHUNK), F32),
        pltpu.VMEM((WIDTH, CHUNK), F32),
        dma((6,)),
        dma,
        dma,
        dma,
        dma,
        dma,
        dma,
        dma((4,)),
        dma((4,)),
        dma,
        dma((TILES,)),
        dma((3,)),
        dma((3,)),
        dma,
        dma((TP,)),
    ]
    return pl.pallas_call(
        mixer_kernel,
        out_shape=jax.ShapeDtypeStruct((CHUNK, WIDTH), BF16),
        in_specs=[pl.BlockSpec(memory_space=pl.ANY)] * 6,
        out_specs=pl.BlockSpec(memory_space=pltpu.VMEM),
        scratch_shapes=scratch,
        compiler_params=pltpu.CompilerParams(
            collective_id=0, has_side_effects=True, vmem_limit_bytes=48 * 1024 * 1024
        ),
        name="mixer",
    )(
        *(
            pltpu.with_memory_space_constraint(array, pltpu.HBM)
            for array in (
                x_gate,
                x_post,
                values,
                jnp.swapaxes(decay, 1, 2),
                jnp.swapaxes(residue, 1, 2),
                w_out,
            )
        )
    )


def solution(mesh):
    in_specs = (
        P("ctx", "tp"),
        P("ctx", "tp"),
        P("ctx", "tp"),
        P(None, "tp", None),
        P(None, "tp", None),
        P(("tp", "ctx"), None),
    )
    return jax.shard_map(
        local, mesh=mesh, in_specs=in_specs, out_specs=P("ctx", "tp"), check_vma=False
    )
```

```python
import jax
import jax.numpy as jnp
from jax import lax
from jax.experimental import pallas as pl
from jax.experimental.pallas import tpu as pltpu
from jax.sharding import PartitionSpec as P

MESH = pl.DeviceIdType.MESH
F32 = jnp.float32
BF16 = jnp.bfloat16
HIGHEST = lax.Precision.HIGHEST

POLES = 16
CHUNK = 128
CHUNKS = 128
CHIPS = 64
OWN = 8
LANES = 128
TILES = 4
TP = 4
WIDTH = TILES * LANES


def far_first():
    def hops(step):
        x, y, z = (min(part, 4 - part) for part in step)
        return x + y + 4 * z

    steps = [(x, y, z) for x in range(4) for y in range(4) for z in range(4)]
    return sorted(steps[1:], key=hops, reverse=True)


STEPS = far_first()


def split(value):
    high = value.astype(BF16)
    return high, (value - high.astype(F32)).astype(BF16)


def matmul(left, right):
    return jnp.dot(left, right, preferred_element_type=F32)


def product3(left, right_high, right_low):
    high, low = split(left)
    return matmul(high, right_high) + (matmul(high, right_low) + matmul(low, right_high))


def mixer_kernel(
    gate_hbm,
    post_hbm,
    vals_hbm,
    decay_hbm,
    residue_hbm,
    w_hbm,
    out_ref,
    gate_s,
    post_s,
    vals_s,
    decay_s,
    residue_s,
    w_s,
    par_own,
    par_out,
    par_in,
    v_out,
    g_out,
    v_in,
    g_in,
    v_rows,
    g_rows,
    post_t,
    table_high,
    table_low,
    back_high,
    back_low,
    rates,
    y_rows,
    o_rows,
    y_give,
    y_take,
    y_out,
    y_in,
    w_planes,
    w_block,
    w_full,
    mix_f32,
    mix,
    acc,
    sums,
    load_sem,
    par_send,
    par_recv,
    v_send,
    v_recv,
    g_send,
    g_recv,
    near_send,
    near_recv,
    out_send,
    out_recv,
    w_send,
    w_recv,
    mix_send,
    mix_recv,
):
    ctx = lax.axis_index("ctx")
    tp = lax.axis_index("tp")
    core = lax.rem(ctx, 2)
    chip = ctx // 2
    z_hi = lax.rem(chip, 4)
    y_pos = lax.rem(chip // 4, 4)
    x_pos = chip // 16
    plane = chip // 4
    sibling = {"ctx": ctx + 1 - 2 * core}
    tp_peers = (tp + 1 - 2 * lax.rem(tp, 2), lax.rem(tp + 2, TP), TP - 1 - tp)

    def moved(step):
        x = lax.rem(x_pos + step[0], 4)
        y = lax.rem(y_pos + step[1], 4)
        z = lax.rem(z_hi + step[2], 4)
        return x * 16 + y * 4 + z

    def same_core(other_chip):
        return {"ctx": other_chip * 2 + core}

    def remote(src, dst, send_sem, recv_sem, device):
        return pltpu.make_async_remote_copy(
            src_ref=src,
            dst_ref=dst,
            send_sem=send_sem,
            recv_sem=recv_sem,
            device_id=device,
            device_id_type=MESH,
        )

    def wait_bytes(ref, sem):
        pltpu.make_async_copy(ref, ref, sem).wait()

    loads = [
        pltpu.make_async_copy(src, dst, load_sem.at[index])
        for index, (src, dst) in enumerate(
            [
                (vals_hbm, vals_s),
                (gate_hbm, gate_s),
                (decay_hbm, decay_s),
                (residue_hbm, residue_s),
                (w_hbm, w_s),
                (post_hbm, post_s),
            ]
        )
    ]
    for load in loads:
        load.start()

    barrier = pltpu.get_barrier_semaphore()
    for step in STEPS:
        pl.semaphore_signal(
            barrier, inc=1, device_id=same_core(moved(step)), device_id_type=MESH
        )
    for other in tp_peers:
        pl.semaphore_signal(barrier, inc=1, device_id={"tp": other}, device_id_type=MESH)
    pl.semaphore_signal(barrier, inc=1, device_id=sibling, device_id_type=MESH)

    def spread(source, target):
        for tile in range(TILES):
            columns = source[:, tile * LANES : (tile + 1) * LANES].astype(F32).T
            for part in range(LANES // OWN):
                target[tile * 16 + part] = columns[part * OWN : (part + 1) * OWN].astype(BF16)

    loads[0].wait()
    spread(vals_s, v_out)
    loads[1].wait()
    spread(gate_s, g_out)

    row_id = lax.broadcasted_iota(jnp.int32, (WIDTH, LANES), 0)
    own_id = lax.broadcasted_iota(jnp.int32, (WIDTH, LANES), 1) // POLES + chip * OWN
    picks = jnp.concatenate(
        [(row_id == own_id).astype(F32), (row_id == WIDTH - 1 - own_id).astype(F32)], axis=1
    )
    pole_mask = (
        lax.broadcasted_iota(jnp.int32, (2, POLES, LANES), 1)
        == lax.rem(lax.broadcasted_iota(jnp.int32, (2, POLES, LANES), 2), POLES)
    ).astype(F32)
    loads[2].wait()
    loads[3].wait()
    par_out[...] = jnp.zeros((8, LANES), F32)
    par_own[...] = jnp.zeros((8, LANES), F32)
    for which, source in enumerate((decay_s, residue_s)):
        both = lax.dot_general(
            source[...].reshape(2 * POLES, WIDTH),
            picks,
            (((1,), (0,)), ((), ())),
            precision=HIGHEST,
            preferred_element_type=F32,
        )
        for target, part in ((par_own, both[:, :LANES]), (par_out, both[:, LANES:])):
            rows = jnp.sum(part.reshape(2, POLES, LANES) * pole_mask, axis=1)
            target[2 * which : 2 * which + 2, :] = rows
    loads[4].wait()
    w_planes[z_hi] = w_s[...]

    pl.semaphore_wait(barrier, len(STEPS) + (TP - 1) + 1)

    par_copy = remote(par_out, par_in, par_send, par_recv, {"tp": TP - 1 - tp})
    par_copy.start()
    for step in STEPS:
        other = moved(step)
        remote(v_out.at[other], v_in.at[chip, core], v_send, v_recv, same_core(other)).start()
    v_in[chip, core] = v_out[chip]

    for offset in (2, 1, 3):
        other = plane * 4 + lax.rem(z_hi + offset, 4)
        remote(
            w_planes.at[z_hi], w_planes.at[z_hi], w_send.at[0], w_recv.at[0], same_core(other)
        ).start()
    for step in STEPS:
        other = moved(step)
        remote(g_out.at[other], g_in.at[chip, core], g_send, g_recv, same_core(other)).start()
    g_in[chip, core] = g_out[chip]

    par_copy.wait_recv()
    poles = jnp.where(core == 1, par_in[...], par_own[...])
    square = (LANES, LANES)
    row = lax.broadcasted_iota(jnp.int32, square, 0)
    col = lax.broadcasted_iota(jnp.int32, square, 1)
    row_f = row.astype(F32)
    reverse = core == 1
    tap_power = jnp.where(reverse, jnp.where(row == 0, 0.0, CHUNK - row_f), row_f)
    out_power = jnp.where(reverse, CHUNK - row_f, row_f + 1.0)
    state_power = jnp.where(reverse, row_f, CHUNK - 1.0 - row_f)
    causal = (col - row) * (1 - 2 * core) >= 0
    channel_mask = (
        lax.broadcasted_iota(jnp.int32, (OWN, LANES), 1) // POLES
        == lax.broadcasted_iota(jnp.int32, (OWN, LANES), 0)
    ).astype(F32)

    def build(filt):
        decay = poles[filt : filt + 1, :]
        weight = poles[2 + filt : 3 + filt, :] * jnp.sqrt(2.0 * decay / POLES)
        rates[filt, 0:1, :] = decay
        taps = lax.dot_general(
            channel_mask,
            weight * jnp.exp(-decay * tap_power),
            (((1,), (1,)), ((), ())),
            precision=HIGHEST,
            preferred_element_type=F32,
        )
        to_states = jnp.exp(-decay * state_power)
        from_states = (weight * jnp.exp(-decay * out_power)).T
        for channel in range(OWN):
            line = jnp.broadcast_to(taps[channel : channel + 1, :], square)
            toeplitz = pltpu.roll(line, 0, 1, stride=1, stride_axis=0)
            high, low = split(jnp.where(causal, toeplitz, 0.0))
            table_high[filt, channel, :, :LANES] = high
            table_low[filt, channel, :, :LANES] = low
            high, low = split(jnp.where(col // POLES == channel, to_states, 0.0))
            table_high[filt, channel, :, LANES:] = high
            table_low[filt, channel, :, LANES:] = low
            high, low = split(jnp.where(row // POLES == channel, from_states, 0.0))
            back_high[filt, channel] = high
            back_low[filt, channel] = low

    build(0)
    build(1)
    loads[5].wait()
    for tile in range(TILES):
        post_t[tile] = post_s[:, tile * LANES : (tile + 1) * LANES].astype(F32).T

    def gather_rows(source, target):
        def body(other, done):
            for half in range(2):
                chunk = other * 2 + half
                place = chunk + core * (CHUNKS - 1 - 2 * chunk)
                rows = pl.ds(pl.multiple_of(place * OWN, OWN), OWN)
                target[rows, :] = source[other, half].astype(F32)
            return done

        lax.fori_loop(0, CHIPS, body, 0, unroll=8)

    def picked(ref, channel):
        return ref[pl.ds(channel, CHUNKS, stride=OWN), :]

    def near(ref, index):
        part = ref.at[:, core]
        return remote(part, part, near_send.at[index], near_recv.at[index], sibling)

    def scan(states, filt):
        decay = rates[filt, 0:1, :]

        def later(value, count):
            return jnp.where(row >= count, pltpu.roll(value, count, 0), 0.0)

        value = later(states, 1)
        for power in range(7):
            count = 2**power
            value = value + jnp.exp(-float(CHUNK * count) * decay) * later(value, count)
        return value

    wait_bytes(w_planes.at[pl.ds(0, 3)], w_recv.at[0])
    for other in range(4):
        w_block[other * 4 : other * 4 + 4, :] = w_planes[other].astype(F32)
    for block in range(TP):
        columns = slice(block * WIDTH, (block + 1) * WIDTH)
        w_full[block, core, x_pos, y_pos] = w_block[:, columns].astype(BF16)
    blocks = (pl.ds(0, 2), pl.ds(2, 2))

    def along(axis, part, sem):
        for offset in (2, 1, 3):
            x = lax.rem(x_pos + offset, 4) if axis == 0 else x_pos
            y = lax.rem(y_pos + offset, 4) if axis == 1 else y_pos
            remote(
                part, part, w_send.at[sem], w_recv.at[sem], same_core(x * 16 + y * 4 + z_hi)
            ).start()

    along(1, w_full.at[blocks[0], core, x_pos, y_pos], 1)
    along(0, w_full.at[blocks[1], core, x_pos, y_pos], 2)

    wait_bytes(v_in.at[pl.ds(0, CHIPS - 1), 0], v_recv)
    v_near = near(v_in, 0)
    v_near.start()
    v_near.wait_recv()
    gather_rows(v_in, v_rows)

    states = jnp.zeros(square, F32)
    for channel in range(OWN):
        line = picked(v_rows, channel).astype(BF16)
        both = matmul(line, table_high[0, channel]) + matmul(line, table_low[0, channel])
        y_rows[channel] = both[:, :LANES]
        states = states + both[:, LANES:]
    carry = scan(states, 0)
    for half in range(2):
        wait_bytes(w_full.at[blocks[half], 0, 0, pl.ds(0, 3)], w_recv.at[1 + half])
    along(0, w_full.at[blocks[0], core, x_pos], 3)
    along(1, w_full.at[blocks[1], core, :, y_pos], 4)
    wait_bytes(g_in.at[pl.ds(0, CHIPS - 1), 0], g_recv)
    g_near = near(g_in, 1)
    g_near.start()
    g_near.wait_recv()
    gather_rows(g_in, g_rows)

    states = jnp.zeros(square, F32)
    for channel in range(OWN):
        value = y_rows[channel] + product3(carry, back_high[0, channel], back_low[0, channel])
        value = value * picked(g_rows, channel)
        both = product3(value, table_high[1, channel], table_low[1, channel])
        y_rows[channel] = both[:, :LANES]
        states = states + both[:, LANES:]
    carry = scan(states, 1)

    y_near = []
    for half in range(2):
        chunks = slice(half * CHIPS, (half + 1) * CHIPS)
        parts = range(half * CHIPS // 2, (half + 1) * CHIPS // 2)
        high, low = split(carry[chunks])
        for channel in range(OWN):
            value = y_rows[channel, chunks, :] + (
                matmul(high, back_high[1, channel])
                + (matmul(high, back_low[1, channel]) + matmul(low, back_high[1, channel]))
            )
            o_rows[pl.ds(half * CHIPS * OWN + channel, CHIPS, stride=OWN), :] = value
        for part in parts:
            y_give[part] = o_rows[(2 * part + 1) * OWN : (2 * part + 2) * OWN, :]
        piece = pl.ds(half * CHIPS // 2, CHIPS // 2)
        copy = remote(
            y_give.at[piece],
            y_take.at[piece],
            near_send.at[2 + half],
            near_recv.at[2 + half],
            sibling,
        )
        copy.start()
        y_near.append(copy)
    for half in (1, 0):
        y_near[1 - half].wait_recv()
        for part in range(half * CHIPS // 2, (half + 1) * CHIPS // 2):
            place = part + core * (CHIPS - 1 - 2 * part)
            total = o_rows[2 * part * OWN : (2 * part + 1) * OWN, :] + y_take[CHIPS - 1 - part]
            y_out[place] = total.astype(BF16)
    for step in STEPS:
        other = moved(step)
        remote(
            y_out.at[other], y_in.at[chip], out_send, out_recv.at[x_pos], same_core(other)
        ).start()
    y_in[chip] = y_out[chip]

    for half in range(2):
        wait_bytes(w_full.at[blocks[half], 0, pl.ds(0, 3)], w_recv.at[3 + half])
    part = w_full.at[:, core]
    w_half = remote(part, part, w_send.at[5], w_recv.at[5], sibling)
    w_half.start()

    for offset in range(TILES):
        tile = lax.rem(x_pos + offset, TILES)
        wait_bytes(y_in.at[pl.ds(0, 15 if offset == 0 else 16)], out_recv.at[tile])
        for part in range(16):
            mix_f32[part * OWN : (part + 1) * OWN, :] = (
                y_in[tile * 16 + part].astype(F32)
                * post_t[tile, part * OWN : (part + 1) * OWN, :]
            )
        rows = pl.ds(pl.multiple_of(tile * LANES, LANES), LANES)
        mix[tp, rows, :] = mix_f32[...].astype(BF16)
        for other in reversed(tp_peers):
            remote(
                mix.at[tp, rows], mix.at[tp, rows], mix_send, mix_recv.at[tp], {"tp": other}
            ).start()

    w_half.wait_recv()

    def project(block):
        return matmul(w_full[block].reshape(WIDTH, WIDTH), mix[block])

    acc[...] = project(tp)
    for block in tp_peers:
        wait_bytes(mix.at[block], mix_recv.at[block])
        acc[...] += project(block)
    for group in range(CHIPS):
        for part in range(2):
            first = part * (WIDTH // 2) + group * 4
            sums[group * 8 + part * 4 : group * 8 + part * 4 + 4, :] = acc[first : first + 4, :]
    for tile in range(TILES):
        rows = slice(tile * LANES, (tile + 1) * LANES)
        out_ref[:, rows] = sums[rows, :].T.astype(BF16)

    par_copy.wait_send()
    wait_bytes(v_in.at[pl.ds(0, CHIPS - 1), 0], v_send)
    wait_bytes(g_in.at[pl.ds(0, CHIPS - 1), 0], g_send)
    v_near.wait_send()
    g_near.wait_send()
    for copy in y_near:
        copy.wait_send()
    wait_bytes(y_in.at[pl.ds(0, CHIPS - 1)], out_send)
    wait_bytes(w_planes.at[pl.ds(0, 3)], w_send.at[0])
    for half in range(2):
        wait_bytes(w_full.at[blocks[half], 0, 0, pl.ds(0, 3)], w_send.at[1 + half])
        wait_bytes(w_full.at[blocks[half], 0, pl.ds(0, 3)], w_send.at[3 + half])
    w_half.wait_send()
    wait_bytes(mix.at[pl.ds(0, TP - 1)], mix_send)


def local(x_gate, x_post, values, decay, residue, w_out):
    dma = pltpu.SemaphoreType.DMA
    scratch = [
        pltpu.VMEM((CHUNK, WIDTH), BF16),
        pltpu.VMEM((CHUNK, WIDTH), BF16),
        pltpu.VMEM((CHUNK, WIDTH), BF16),
        pltpu.VMEM((2, POLES, WIDTH), F32),
        pltpu.VMEM((2, POLES, WIDTH), F32),
        pltpu.VMEM((4, TP * WIDTH), BF16),
        pltpu.VMEM((8, LANES), F32),
        pltpu.VMEM((8, LANES), F32),
        pltpu.VMEM((8, LANES), F32),
        pltpu.VMEM((CHIPS, OWN, CHUNK), BF16),
        pltpu.VMEM((CHIPS, OWN, CHUNK), BF16),
        pltpu.VMEM((CHIPS, 2, OWN, CHUNK), BF16),
        pltpu.VMEM((CHIPS, 2, OWN, CHUNK), BF16),
        pltpu.VMEM((CHUNKS * OWN, CHUNK), F32),
        pltpu.VMEM((CHUNKS * OWN, CHUNK), F32),
        pltpu.VMEM((TILES, LANES, CHUNK), F32),
        pltpu.VMEM((2, OWN, CHUNK, 2 * LANES), BF16),
        pltpu.VMEM((2, OWN, CHUNK, 2 * LANES), BF16),
        pltpu.VMEM((2, OWN, LANES, CHUNK), BF16),
        pltpu.VMEM((2, OWN, LANES, CHUNK), BF16),
        pltpu.VMEM((2, 8, LANES), F32),
        pltpu.VMEM((OWN, CHUNKS, CHUNK), F32),
        pltpu.VMEM((CHUNKS * OWN, CHUNK), F32),
        pltpu.VMEM((CHIPS, OWN, CHUNK), F32),
        pltpu.VMEM((CHIPS, OWN, CHUNK), F32),
        pltpu.VMEM((CHIPS, OWN, CHUNK), BF16),
        pltpu.VMEM((CHIPS, OWN, CHUNK), BF16),
        pltpu.VMEM((4, 4, TP * WIDTH), BF16),
        pltpu.VMEM((16, TP * WIDTH), F32),
        pltpu.VMEM((TP, 2, 4, 4, 16, WIDTH), BF16),
        pltpu.VMEM((LANES, CHUNK), F32),
        pltpu.VMEM((TP, WIDTH, CHUNK), BF16),
        pltpu.VMEM((WIDTH, CHUNK), F32),
        pltpu.VMEM((WIDTH, CHUNK), F32),
        dma((6,)),
        dma,
        dma,
        dma,
        dma,
        dma,
        dma,
        dma((4,)),
        dma((4,)),
        dma,
        dma((TILES,)),
        dma((6,)),
        dma((6,)),
        dma,
        dma((TP,)),
    ]
    return pl.pallas_call(
        mixer_kernel,
        out_shape=jax.ShapeDtypeStruct((CHUNK, WIDTH), BF16),
        in_specs=[pl.BlockSpec(memory_space=pl.ANY)] * 6,
        out_specs=pl.BlockSpec(memory_space=pltpu.VMEM),
        scratch_shapes=scratch,
        compiler_params=pltpu.CompilerParams(
            collective_id=0, has_side_effects=True, vmem_limit_bytes=48 * 1024 * 1024
        ),
        name="mixer",
    )(
        *(
            pltpu.with_memory_space_constraint(array, pltpu.HBM)
            for array in (
                x_gate,
                x_post,
                values,
                jnp.swapaxes(decay, 1, 2),
                jnp.swapaxes(residue, 1, 2),
                w_out,
            )
        )
    )


def solution(mesh):
    in_specs = (
        P("ctx", "tp"),
        P("ctx", "tp"),
        P("ctx", "tp"),
        P(None, "tp", None),
        P(None, "tp", None),
        P(("tp", "ctx"), None),
    )
    return jax.shard_map(
        local, mesh=mesh, in_specs=in_specs, out_specs=P("ctx", "tp"), check_vma=False
    )
```

```python
import jax
import jax.numpy as jnp
from jax import lax
from jax.experimental import pallas as pl
from jax.experimental.pallas import tpu as pltpu
from jax.sharding import PartitionSpec as P

MESH = pl.DeviceIdType.MESH
F32 = jnp.float32
BF16 = jnp.bfloat16
HIGHEST = lax.Precision.HIGHEST

POLES = 16
CHUNK = 128
CHUNKS = 128
CHIPS = 64
OWN = 8
LANES = 128
TILES = 4
TP = 4
WIDTH = TILES * LANES


def far_first():
    def hops(step):
        x, y, z = (min(part, 4 - part) for part in step)
        return x + y + 4 * z

    steps = [(x, y, z) for x in range(4) for y in range(4) for z in range(4)]
    return sorted(steps[1:], key=hops, reverse=True)


STEPS = far_first()


def split(value):
    high = value.astype(BF16)
    return high, (value - high.astype(F32)).astype(BF16)


def matmul(left, right):
    return jnp.dot(left, right, preferred_element_type=F32)


def product3(left, right_high, right_low):
    high, low = split(left)
    return matmul(high, right_high) + (matmul(high, right_low) + matmul(low, right_high))


def mixer_kernel(
    gate_hbm,
    post_hbm,
    vals_hbm,
    decay_hbm,
    residue_hbm,
    w_hbm,
    out_ref,
    gate_s,
    post_s,
    vals_s,
    decay_s,
    residue_s,
    w_s,
    par_own,
    par_out,
    par_in,
    v_out,
    g_out,
    v_in,
    g_in,
    v_rows,
    g_rows,
    post_t,
    table_high,
    table_low,
    back_high,
    back_low,
    rates,
    y_rows,
    o_rows,
    y_give,
    y_take,
    y_out,
    y_in,
    w_planes,
    w_block,
    w_full,
    mix_f32,
    mix,
    acc,
    sums,
    load_sem,
    par_send,
    par_recv,
    v_send,
    v_recv,
    g_send,
    g_recv,
    near_send,
    near_recv,
    out_send,
    out_recv,
    w_send,
    w_recv,
    mix_send,
    mix_recv,
):
    ctx = lax.axis_index("ctx")
    tp = lax.axis_index("tp")
    core = lax.rem(ctx, 2)
    chip = ctx // 2
    z_hi = lax.rem(chip, 4)
    y_pos = lax.rem(chip // 4, 4)
    x_pos = chip // 16
    plane = chip // 4
    sibling = {"ctx": ctx + 1 - 2 * core}
    tp_peers = (tp + 1 - 2 * lax.rem(tp, 2), lax.rem(tp + 2, TP), TP - 1 - tp)

    def moved(step):
        x = lax.rem(x_pos + step[0], 4)
        y = lax.rem(y_pos + step[1], 4)
        z = lax.rem(z_hi + step[2], 4)
        return x * 16 + y * 4 + z

    def same_core(other_chip):
        return {"ctx": other_chip * 2 + core}

    def remote(src, dst, send_sem, recv_sem, device):
        return pltpu.make_async_remote_copy(
            src_ref=src,
            dst_ref=dst,
            send_sem=send_sem,
            recv_sem=recv_sem,
            device_id=device,
            device_id_type=MESH,
        )

    def wait_bytes(ref, sem):
        pltpu.make_async_copy(ref, ref, sem).wait()

    loads = [
        pltpu.make_async_copy(src, dst, load_sem.at[index])
        for index, (src, dst) in enumerate(
            [
                (vals_hbm, vals_s),
                (gate_hbm, gate_s),
                (decay_hbm, decay_s),
                (residue_hbm, residue_s),
                (w_hbm, w_s),
                (post_hbm, post_s),
            ]
        )
    ]
    barrier = pltpu.get_barrier_semaphore()
    for step in STEPS:
        pl.semaphore_signal(
            barrier, inc=1, device_id=same_core(moved(step)), device_id_type=MESH
        )
    for other in tp_peers:
        pl.semaphore_signal(barrier, inc=1, device_id={"tp": other}, device_id_type=MESH)
    pl.semaphore_signal(barrier, inc=1, device_id=sibling, device_id_type=MESH)
    for load in loads:
        load.start()

    def spread(source, target):
        for tile in range(TILES):
            columns = source[:, tile * LANES : (tile + 1) * LANES].astype(F32).T
            for part in range(LANES // OWN):
                target[tile * 16 + part] = columns[part * OWN : (part + 1) * OWN].astype(BF16)

    loads[0].wait()
    spread(vals_s, v_out)
    loads[1].wait()
    spread(gate_s, g_out)

    row_id = lax.broadcasted_iota(jnp.int32, (WIDTH, LANES), 0)
    own_id = lax.broadcasted_iota(jnp.int32, (WIDTH, LANES), 1) // POLES + chip * OWN
    picks = jnp.concatenate(
        [(row_id == own_id).astype(F32), (row_id == WIDTH - 1 - own_id).astype(F32)], axis=1
    )
    pole_mask = (
        lax.broadcasted_iota(jnp.int32, (2, POLES, LANES), 1)
        == lax.rem(lax.broadcasted_iota(jnp.int32, (2, POLES, LANES), 2), POLES)
    ).astype(F32)
    loads[2].wait()
    loads[3].wait()
    par_out[...] = jnp.zeros((8, LANES), F32)
    par_own[...] = jnp.zeros((8, LANES), F32)
    for which, source in enumerate((decay_s, residue_s)):
        both = lax.dot_general(
            source[...].reshape(2 * POLES, WIDTH),
            picks,
            (((1,), (0,)), ((), ())),
            precision=HIGHEST,
            preferred_element_type=F32,
        )
        for target, part in ((par_own, both[:, :LANES]), (par_out, both[:, LANES:])):
            rows = jnp.sum(part.reshape(2, POLES, LANES) * pole_mask, axis=1)
            target[2 * which : 2 * which + 2, :] = rows
    loads[4].wait()
    w_planes[z_hi] = w_s[...]

    pl.semaphore_wait(barrier, len(STEPS) + (TP - 1) + 1)

    par_copy = remote(par_out, par_in, par_send, par_recv, {"tp": TP - 1 - tp})
    par_copy.start()
    for step in STEPS:
        other = moved(step)
        remote(v_out.at[other], v_in.at[chip, core], v_send, v_recv, same_core(other)).start()
    v_in[chip, core] = v_out[chip]

    for offset in (2, 1, 3):
        other = plane * 4 + lax.rem(z_hi + offset, 4)
        remote(
            w_planes.at[z_hi], w_planes.at[z_hi], w_send.at[0], w_recv.at[0], same_core(other)
        ).start()
    for step in STEPS:
        other = moved(step)
        remote(g_out.at[other], g_in.at[chip, core], g_send, g_recv, same_core(other)).start()
    g_in[chip, core] = g_out[chip]

    par_copy.wait_recv()
    poles = jnp.where(core == 1, par_in[...], par_own[...])
    square = (LANES, LANES)
    row = lax.broadcasted_iota(jnp.int32, square, 0)
    col = lax.broadcasted_iota(jnp.int32, square, 1)
    row_f = row.astype(F32)
    reverse = core == 1
    tap_power = jnp.where(reverse, jnp.where(row == 0, 0.0, CHUNK - row_f), row_f)
    out_power = jnp.where(reverse, CHUNK - row_f, row_f + 1.0)
    state_power = jnp.where(reverse, row_f, CHUNK - 1.0 - row_f)
    causal = (col - row) * (1 - 2 * core) >= 0
    channel_mask = (
        lax.broadcasted_iota(jnp.int32, (OWN, LANES), 1) // POLES
        == lax.broadcasted_iota(jnp.int32, (OWN, LANES), 0)
    ).astype(F32)

    def build(filt):
        decay = poles[filt : filt + 1, :]
        weight = poles[2 + filt : 3 + filt, :] * jnp.sqrt(2.0 * decay / POLES)
        rates[filt, 0:1, :] = decay
        taps = lax.dot_general(
            channel_mask,
            weight * jnp.exp(-decay * tap_power),
            (((1,), (1,)), ((), ())),
            precision=HIGHEST,
            preferred_element_type=F32,
        )
        to_states = jnp.exp(-decay * state_power)
        from_states = (weight * jnp.exp(-decay * out_power)).T
        for channel in range(OWN):
            line = jnp.broadcast_to(taps[channel : channel + 1, :], square)
            toeplitz = pltpu.roll(line, 0, 1, stride=1, stride_axis=0)
            high, low = split(jnp.where(causal, toeplitz, 0.0))
            table_high[filt, channel, :, :LANES] = high
            table_low[filt, channel, :, :LANES] = low
            high, low = split(jnp.where(col // POLES == channel, to_states, 0.0))
            table_high[filt, channel, :, LANES:] = high
            table_low[filt, channel, :, LANES:] = low
            high, low = split(jnp.where(row // POLES == channel, from_states, 0.0))
            back_high[filt, channel] = high
            back_low[filt, channel] = low

    build(0)
    build(1)
    loads[5].wait()
    for tile in range(TILES):
        post_t[tile] = post_s[:, tile * LANES : (tile + 1) * LANES].astype(F32).T

    def gather_rows(source, target):
        def body(other, done):
            for half in range(2):
                chunk = other * 2 + half
                place = chunk + core * (CHUNKS - 1 - 2 * chunk)
                rows = pl.ds(pl.multiple_of(place * OWN, OWN), OWN)
                target[rows, :] = source[other, half].astype(F32)
            return done

        lax.fori_loop(0, CHIPS, body, 0, unroll=8)

    def picked(ref, channel):
        return ref[pl.ds(channel, CHUNKS, stride=OWN), :]

    def near(ref, index):
        part = ref.at[:, core]
        return remote(part, part, near_send.at[index], near_recv.at[index], sibling)

    def scan(states, filt):
        decay = rates[filt, 0:1, :]

        def later(value, count):
            return jnp.where(row >= count, pltpu.roll(value, count, 0), 0.0)

        value = later(states, 1)
        for power in range(7):
            count = 2**power
            value = value + jnp.exp(-float(CHUNK * count) * decay) * later(value, count)
        return value

    wait_bytes(w_planes.at[pl.ds(0, 3)], w_recv.at[0])
    for other in range(4):
        w_block[other * 4 : other * 4 + 4, :] = w_planes[other].astype(F32)
    for block in range(TP):
        columns = slice(block * WIDTH, (block + 1) * WIDTH)
        w_full[block, core, x_pos, y_pos] = w_block[:, columns].astype(BF16)
    blocks = (pl.ds(0, 2), pl.ds(2, 2))

    def along(axis, part, sem):
        for offset in (2, 1, 3):
            x = lax.rem(x_pos + offset, 4) if axis == 0 else x_pos
            y = lax.rem(y_pos + offset, 4) if axis == 1 else y_pos
            remote(
                part, part, w_send.at[sem], w_recv.at[sem], same_core(x * 16 + y * 4 + z_hi)
            ).start()

    along(1, w_full.at[blocks[0], core, x_pos, y_pos], 1)
    along(0, w_full.at[blocks[1], core, x_pos, y_pos], 2)

    wait_bytes(v_in.at[pl.ds(0, CHIPS - 1), 0], v_recv)
    v_near = near(v_in, 0)
    v_near.start()
    v_near.wait_recv()
    gather_rows(v_in, v_rows)

    states = jnp.zeros(square, F32)
    for channel in range(OWN):
        line = picked(v_rows, channel).astype(BF16)
        both = matmul(line, table_high[0, channel]) + matmul(line, table_low[0, channel])
        y_rows[channel] = both[:, :LANES]
        states = states + both[:, LANES:]
    carry = scan(states, 0)
    for half in range(2):
        wait_bytes(w_full.at[blocks[half], 0, 0, pl.ds(0, 3)], w_recv.at[1 + half])
    along(0, w_full.at[blocks[0], core, x_pos], 3)
    along(1, w_full.at[blocks[1], core, :, y_pos], 4)
    wait_bytes(g_in.at[pl.ds(0, CHIPS - 1), 0], g_recv)
    g_near = near(g_in, 1)
    g_near.start()
    g_near.wait_recv()
    gather_rows(g_in, g_rows)

    states = jnp.zeros(square, F32)
    for channel in range(OWN):
        value = y_rows[channel] + product3(carry, back_high[0, channel], back_low[0, channel])
        value = value * picked(g_rows, channel)
        both = product3(value, table_high[1, channel], table_low[1, channel])
        y_rows[channel] = both[:, :LANES]
        states = states + both[:, LANES:]
    carry = scan(states, 1)

    y_near = []
    for half in range(2):
        chunks = slice(half * CHIPS, (half + 1) * CHIPS)
        parts = range(half * CHIPS // 2, (half + 1) * CHIPS // 2)
        high, low = split(carry[chunks])
        for channel in range(OWN):
            value = y_rows[channel, chunks, :] + (
                matmul(high, back_high[1, channel])
                + (matmul(high, back_low[1, channel]) + matmul(low, back_high[1, channel]))
            )
            o_rows[pl.ds(half * CHIPS * OWN + channel, CHIPS, stride=OWN), :] = value
        for part in parts:
            y_give[part] = o_rows[(2 * part + 1) * OWN : (2 * part + 2) * OWN, :]
        piece = pl.ds(half * CHIPS // 2, CHIPS // 2)
        copy = remote(
            y_give.at[piece],
            y_take.at[piece],
            near_send.at[2 + half],
            near_recv.at[2 + half],
            sibling,
        )
        copy.start()
        y_near.append(copy)
    for half in (1, 0):
        y_near[1 - half].wait_recv()
        for part in range(half * CHIPS // 2, (half + 1) * CHIPS // 2):
            place = part + core * (CHIPS - 1 - 2 * part)
            total = o_rows[2 * part * OWN : (2 * part + 1) * OWN, :] + y_take[CHIPS - 1 - part]
            y_out[place] = total.astype(BF16)
    for step in STEPS:
        other = moved(step)
        remote(
            y_out.at[other], y_in.at[chip], out_send, out_recv.at[x_pos], same_core(other)
        ).start()
    y_in[chip] = y_out[chip]

    for half in range(2):
        wait_bytes(w_full.at[blocks[half], 0, pl.ds(0, 3)], w_recv.at[3 + half])
    part = w_full.at[:, core]
    w_half = remote(part, part, w_send.at[5], w_recv.at[5], sibling)
    w_half.start()

    for offset in range(TILES):
        tile = lax.rem(x_pos + offset, TILES)
        wait_bytes(y_in.at[pl.ds(0, 15 if offset == 0 else 16)], out_recv.at[tile])
        for part in range(16):
            mix_f32[part * OWN : (part + 1) * OWN, :] = (
                y_in[tile * 16 + part].astype(F32)
                * post_t[tile, part * OWN : (part + 1) * OWN, :]
            )
        rows = pl.ds(pl.multiple_of(tile * LANES, LANES), LANES)
        mix[tp, rows, :] = mix_f32[...].astype(BF16)
        part = mix.at[tp, rows]
        remote(part, part, mix_send, mix_recv.at[2 + tile], {"tp": tp_peers[1]}).start()
        remote(part, part, mix_send, mix_recv.at[0], {"tp": tp_peers[0]}).start()

    def project(block):
        return matmul(w_full[block].reshape(WIDTH, WIDTH), mix[block])

    w_half.wait_recv()
    acc[...] = project(tp)
    for offset in range(TILES):
        tile = lax.rem(x_pos + offset, TILES)
        part = mix.at[tp_peers[1], pl.ds(pl.multiple_of(tile * LANES, LANES), LANES)]
        wait_bytes(part, mix_recv.at[2 + tile])
        remote(part, part, mix_send, mix_recv.at[1], {"tp": tp_peers[0]}).start()
    acc[...] += project(tp_peers[1])
    wait_bytes(mix.at[tp_peers[0]], mix_recv.at[0])
    acc[...] += project(tp_peers[0])
    wait_bytes(mix.at[tp_peers[2]], mix_recv.at[1])
    acc[...] += project(tp_peers[2])
    for group in range(CHIPS):
        for part in range(2):
            first = part * (WIDTH // 2) + group * 4
            sums[group * 8 + part * 4 : group * 8 + part * 4 + 4, :] = acc[first : first + 4, :]
    for tile in range(TILES):
        rows = slice(tile * LANES, (tile + 1) * LANES)
        out_ref[:, rows] = sums[rows, :].T.astype(BF16)

    par_copy.wait_send()
    wait_bytes(v_in.at[pl.ds(0, CHIPS - 1), 0], v_send)
    wait_bytes(g_in.at[pl.ds(0, CHIPS - 1), 0], g_send)
    v_near.wait_send()
    g_near.wait_send()
    for copy in y_near:
        copy.wait_send()
    wait_bytes(y_in.at[pl.ds(0, CHIPS - 1)], out_send)
    wait_bytes(w_planes.at[pl.ds(0, 3)], w_send.at[0])
    for half in range(2):
        wait_bytes(w_full.at[blocks[half], 0, 0, pl.ds(0, 3)], w_send.at[1 + half])
        wait_bytes(w_full.at[blocks[half], 0, pl.ds(0, 3)], w_send.at[3 + half])
    w_half.wait_send()
    wait_bytes(mix.at[pl.ds(0, TP - 1)], mix_send)


def local(x_gate, x_post, values, decay, residue, w_out):
    dma = pltpu.SemaphoreType.DMA
    scratch = [
        pltpu.VMEM((CHUNK, WIDTH), BF16),
        pltpu.VMEM((CHUNK, WIDTH), BF16),
        pltpu.VMEM((CHUNK, WIDTH), BF16),
        pltpu.VMEM((2, POLES, WIDTH), F32),
        pltpu.VMEM((2, POLES, WIDTH), F32),
        pltpu.VMEM((4, TP * WIDTH), BF16),
        pltpu.VMEM((8, LANES), F32),
        pltpu.VMEM((8, LANES), F32),
        pltpu.VMEM((8, LANES), F32),
        pltpu.VMEM((CHIPS, OWN, CHUNK), BF16),
        pltpu.VMEM((CHIPS, OWN, CHUNK), BF16),
        pltpu.VMEM((CHIPS, 2, OWN, CHUNK), BF16),
        pltpu.VMEM((CHIPS, 2, OWN, CHUNK), BF16),
        pltpu.VMEM((CHUNKS * OWN, CHUNK), F32),
        pltpu.VMEM((CHUNKS * OWN, CHUNK), F32),
        pltpu.VMEM((TILES, LANES, CHUNK), F32),
        pltpu.VMEM((2, OWN, CHUNK, 2 * LANES), BF16),
        pltpu.VMEM((2, OWN, CHUNK, 2 * LANES), BF16),
        pltpu.VMEM((2, OWN, LANES, CHUNK), BF16),
        pltpu.VMEM((2, OWN, LANES, CHUNK), BF16),
        pltpu.VMEM((2, 8, LANES), F32),
        pltpu.VMEM((OWN, CHUNKS, CHUNK), F32),
        pltpu.VMEM((CHUNKS * OWN, CHUNK), F32),
        pltpu.VMEM((CHIPS, OWN, CHUNK), F32),
        pltpu.VMEM((CHIPS, OWN, CHUNK), F32),
        pltpu.VMEM((CHIPS, OWN, CHUNK), BF16),
        pltpu.VMEM((CHIPS, OWN, CHUNK), BF16),
        pltpu.VMEM((4, 4, TP * WIDTH), BF16),
        pltpu.VMEM((16, TP * WIDTH), F32),
        pltpu.VMEM((TP, 2, 4, 4, 16, WIDTH), BF16),
        pltpu.VMEM((LANES, CHUNK), F32),
        pltpu.VMEM((TP, WIDTH, CHUNK), BF16),
        pltpu.VMEM((WIDTH, CHUNK), F32),
        pltpu.VMEM((WIDTH, CHUNK), F32),
        dma((6,)),
        dma,
        dma,
        dma,
        dma,
        dma,
        dma,
        dma((4,)),
        dma((4,)),
        dma,
        dma((TILES,)),
        dma((6,)),
        dma((6,)),
        dma,
        dma((2 + TILES,)),
    ]
    return pl.pallas_call(
        mixer_kernel,
        out_shape=jax.ShapeDtypeStruct((CHUNK, WIDTH), BF16),
        in_specs=[pl.BlockSpec(memory_space=pl.ANY)] * 6,
        out_specs=pl.BlockSpec(memory_space=pltpu.VMEM),
        scratch_shapes=scratch,
        compiler_params=pltpu.CompilerParams(
            collective_id=0, has_side_effects=True, vmem_limit_bytes=48 * 1024 * 1024
        ),
        name="mixer",
    )(
        *(
            pltpu.with_memory_space_constraint(array, pltpu.HBM)
            for array in (
                x_gate,
                x_post,
                values,
                jnp.swapaxes(decay, 1, 2),
                jnp.swapaxes(residue, 1, 2),
                w_out,
            )
        )
    )


def solution(mesh):
    in_specs = (
        P("ctx", "tp"),
        P("ctx", "tp"),
        P("ctx", "tp"),
        P(None, "tp", None),
        P(None, "tp", None),
        P(("tp", "ctx"), None),
    )
    return jax.shard_map(
        local, mesh=mesh, in_specs=in_specs, out_specs=P("ctx", "tp"), check_vma=False
    )
```

```python
import jax
import jax.numpy as jnp
from jax import lax
from jax.experimental import pallas as pl
from jax.experimental.pallas import tpu as pltpu
from jax.sharding import PartitionSpec as P

MESH = pl.DeviceIdType.MESH
F32 = jnp.float32
BF16 = jnp.bfloat16
HIGHEST = lax.Precision.HIGHEST

POLES = 16
CHUNK = 128
CHUNKS = 128
CHIPS = 64
OWN = 8
LANES = 128
TILES = 4
TP = 4
WIDTH = TILES * LANES


def far_first():
    def hops(step):
        x, y, z = (min(part, 4 - part) for part in step)
        return x + y + 4 * z

    steps = [(x, y, z) for x in range(4) for y in range(4) for z in range(4)]
    return sorted(steps[1:], key=hops, reverse=True)


STEPS = far_first()


def split(value):
    high = value.astype(BF16)
    return high, (value - high.astype(F32)).astype(BF16)


def matmul(left, right):
    return jnp.dot(left, right, preferred_element_type=F32)


def product3(left, right_high, right_low):
    high, low = split(left)
    return matmul(high, right_high) + (matmul(high, right_low) + matmul(low, right_high))


def mixer_kernel(
    gate_hbm,
    post_hbm,
    vals_hbm,
    decay_hbm,
    residue_hbm,
    w_hbm,
    out_ref,
    gate_s,
    post_s,
    vals_s,
    decay_s,
    residue_s,
    w_s,
    par_own,
    par_out,
    par_in,
    v_out,
    g_out,
    v_in,
    g_in,
    v_rows,
    g_rows,
    post_t,
    table_high,
    table_low,
    back_high,
    back_low,
    rates,
    y_rows,
    o_rows,
    y_give,
    y_take,
    y_out,
    y_in,
    w_planes,
    w_block,
    w_full,
    mix_f32,
    mix,
    acc,
    sums,
    load_sem,
    par_send,
    par_recv,
    v_send,
    v_recv,
    g_send,
    g_recv,
    near_send,
    near_recv,
    out_send,
    out_recv,
    w_send,
    w_recv,
    mix_send,
    mix_recv,
):
    ctx = lax.axis_index("ctx")
    tp = lax.axis_index("tp")
    core = lax.rem(ctx, 2)
    chip = ctx // 2
    z_hi = lax.rem(chip, 4)
    y_pos = lax.rem(chip // 4, 4)
    x_pos = chip // 16
    plane = chip // 4
    sibling = {"ctx": ctx + 1 - 2 * core}
    tp_peers = (tp + 1 - 2 * lax.rem(tp, 2), lax.rem(tp + 2, TP), TP - 1 - tp)

    def moved(step):
        x = lax.rem(x_pos + step[0], 4)
        y = lax.rem(y_pos + step[1], 4)
        z = lax.rem(z_hi + step[2], 4)
        return x * 16 + y * 4 + z

    def same_core(other_chip):
        return {"ctx": other_chip * 2 + core}

    def remote(src, dst, send_sem, recv_sem, device):
        return pltpu.make_async_remote_copy(
            src_ref=src,
            dst_ref=dst,
            send_sem=send_sem,
            recv_sem=recv_sem,
            device_id=device,
            device_id_type=MESH,
        )

    def wait_bytes(ref, sem):
        pltpu.make_async_copy(ref, ref, sem).wait()

    loads = [
        pltpu.make_async_copy(src, dst, load_sem.at[index])
        for index, (src, dst) in enumerate(
            [
                (vals_hbm, vals_s),
                (gate_hbm, gate_s),
                (decay_hbm, decay_s),
                (residue_hbm, residue_s),
                (w_hbm, w_s),
                (post_hbm, post_s),
            ]
        )
    ]
    barrier = pltpu.get_barrier_semaphore()
    for step in STEPS:
        pl.semaphore_signal(
            barrier, inc=1, device_id=same_core(moved(step)), device_id_type=MESH
        )
    for other in tp_peers:
        pl.semaphore_signal(barrier, inc=1, device_id={"tp": other}, device_id_type=MESH)
    pl.semaphore_signal(barrier, inc=1, device_id=sibling, device_id_type=MESH)
    for load in loads:
        load.start()

    def spread(source, target):
        for tile in range(TILES):
            columns = source[:, tile * LANES : (tile + 1) * LANES].astype(F32).T
            for part in range(LANES // OWN):
                target[tile * 16 + part] = columns[part * OWN : (part + 1) * OWN].astype(BF16)

    loads[0].wait()
    spread(vals_s, v_out)
    loads[1].wait()
    spread(gate_s, g_out)

    row_id = lax.broadcasted_iota(jnp.int32, (WIDTH, LANES), 0)
    own_id = lax.broadcasted_iota(jnp.int32, (WIDTH, LANES), 1) // POLES + chip * OWN
    picks = jnp.concatenate(
        [(row_id == own_id).astype(F32), (row_id == WIDTH - 1 - own_id).astype(F32)], axis=1
    )
    pole_mask = (
        lax.broadcasted_iota(jnp.int32, (2, POLES, LANES), 1)
        == lax.rem(lax.broadcasted_iota(jnp.int32, (2, POLES, LANES), 2), POLES)
    ).astype(F32)
    loads[2].wait()
    loads[3].wait()
    par_out[...] = jnp.zeros((8, LANES), F32)
    par_own[...] = jnp.zeros((8, LANES), F32)
    for which, source in enumerate((decay_s, residue_s)):
        both = lax.dot_general(
            source[...].reshape(2 * POLES, WIDTH),
            picks,
            (((1,), (0,)), ((), ())),
            precision=HIGHEST,
            preferred_element_type=F32,
        )
        for target, part in ((par_own, both[:, :LANES]), (par_out, both[:, LANES:])):
            rows = jnp.sum(part.reshape(2, POLES, LANES) * pole_mask, axis=1)
            target[2 * which : 2 * which + 2, :] = rows
    loads[4].wait()
    w_planes[z_hi] = w_s[...]

    pl.semaphore_wait(barrier, len(STEPS) + (TP - 1) + 1)

    par_copy = remote(par_out, par_in, par_send, par_recv, {"tp": TP - 1 - tp})
    par_copy.start()
    for step in STEPS:
        other = moved(step)
        remote(v_out.at[other], v_in.at[chip, core], v_send, v_recv, same_core(other)).start()
    v_in[chip, core] = v_out[chip]

    for step in STEPS:
        other = moved(step)
        remote(g_out.at[other], g_in.at[chip, core], g_send, g_recv, same_core(other)).start()
    g_in[chip, core] = g_out[chip]

    for offset in (2, 1, 3):
        other = plane * 4 + lax.rem(z_hi + offset, 4)
        remote(
            w_planes.at[z_hi], w_planes.at[z_hi], w_send.at[0], w_recv.at[0], same_core(other)
        ).start()

    par_copy.wait_recv()
    poles = jnp.where(core == 1, par_in[...], par_own[...])
    square = (LANES, LANES)
    row = lax.broadcasted_iota(jnp.int32, square, 0)
    col = lax.broadcasted_iota(jnp.int32, square, 1)
    row_f = row.astype(F32)
    reverse = core == 1
    tap_power = jnp.where(reverse, jnp.where(row == 0, 0.0, CHUNK - row_f), row_f)
    out_power = jnp.where(reverse, CHUNK - row_f, row_f + 1.0)
    state_power = jnp.where(reverse, row_f, CHUNK - 1.0 - row_f)
    causal = (col - row) * (1 - 2 * core) >= 0
    channel_mask = (
        lax.broadcasted_iota(jnp.int32, (OWN, LANES), 1) // POLES
        == lax.broadcasted_iota(jnp.int32, (OWN, LANES), 0)
    ).astype(F32)

    def build(filt):
        decay = poles[filt : filt + 1, :]
        weight = poles[2 + filt : 3 + filt, :] * jnp.sqrt(2.0 * decay / POLES)
        rates[filt, 0:1, :] = decay
        taps = lax.dot_general(
            channel_mask,
            weight * jnp.exp(-decay * tap_power),
            (((1,), (1,)), ((), ())),
            precision=HIGHEST,
            preferred_element_type=F32,
        )
        to_states = jnp.exp(-decay * state_power)
        from_states = (weight * jnp.exp(-decay * out_power)).T
        for channel in range(OWN):
            line = jnp.broadcast_to(taps[channel : channel + 1, :], square)
            toeplitz = pltpu.roll(line, 0, 1, stride=1, stride_axis=0)
            high, low = split(jnp.where(causal, toeplitz, 0.0))
            table_high[filt, channel, :, :LANES] = high
            table_low[filt, channel, :, :LANES] = low
            high, low = split(jnp.where(col // POLES == channel, to_states, 0.0))
            table_high[filt, channel, :, LANES:] = high
            table_low[filt, channel, :, LANES:] = low
            high, low = split(jnp.where(row // POLES == channel, from_states, 0.0))
            back_high[filt, channel] = high
            back_low[filt, channel] = low

    build(0)
    build(1)
    loads[5].wait()
    for tile in range(TILES):
        post_t[tile] = post_s[:, tile * LANES : (tile + 1) * LANES].astype(F32).T

    def gather_rows(source, target):
        def body(other, done):
            for half in range(2):
                chunk = other * 2 + half
                place = chunk + core * (CHUNKS - 1 - 2 * chunk)
                rows = pl.ds(pl.multiple_of(place * OWN, OWN), OWN)
                target[rows, :] = source[other, half].astype(F32)
            return done

        lax.fori_loop(0, CHIPS, body, 0, unroll=8)

    def picked(ref, channel):
        return ref[pl.ds(channel, CHUNKS, stride=OWN), :]

    def near(ref, index):
        part = ref.at[:, core]
        return remote(part, part, near_send.at[index], near_recv.at[index], sibling)

    def scan(states, filt):
        decay = rates[filt, 0:1, :]

        def later(value, count):
            return jnp.where(row >= count, pltpu.roll(value, count, 0), 0.0)

        value = later(states, 1)
        for power in range(7):
            count = 2**power
            value = value + jnp.exp(-float(CHUNK * count) * decay) * later(value, count)
        return value

    wait_bytes(v_in.at[pl.ds(0, CHIPS - 1), 0], v_recv)
    v_near = near(v_in, 0)
    v_near.start()
    v_near.wait_recv()
    gather_rows(v_in, v_rows)

    states = jnp.zeros(square, F32)
    for channel in range(OWN):
        line = picked(v_rows, channel).astype(BF16)
        both = matmul(line, table_high[0, channel]) + matmul(line, table_low[0, channel])
        y_rows[channel] = both[:, :LANES]
        states = states + both[:, LANES:]
    carry = scan(states, 0)
    wait_bytes(g_in.at[pl.ds(0, CHIPS - 1), 0], g_recv)
    g_near = near(g_in, 1)
    g_near.start()

    g_near.wait_recv()
    gather_rows(g_in, g_rows)

    states = jnp.zeros(square, F32)
    for channel in range(OWN):
        value = y_rows[channel] + product3(carry, back_high[0, channel], back_low[0, channel])
        value = value * picked(g_rows, channel)
        both = product3(value, table_high[1, channel], table_low[1, channel])
        y_rows[channel] = both[:, :LANES]
        states = states + both[:, LANES:]
    wait_bytes(w_planes.at[pl.ds(0, 3)], w_recv.at[0])
    for other in range(4):
        w_block[other * 4 : other * 4 + 4, :] = w_planes[other].astype(F32)
    for block in range(TP):
        columns = slice(block * WIDTH, (block + 1) * WIDTH)
        w_full[block, core, x_pos, y_pos] = w_block[:, columns].astype(BF16)
    blocks = (pl.ds(0, 2), pl.ds(2, 2))

    def along(axis, part, sem):
        for offset in (2, 1, 3):
            x = lax.rem(x_pos + offset, 4) if axis == 0 else x_pos
            y = lax.rem(y_pos + offset, 4) if axis == 1 else y_pos
            remote(
                part, part, w_send.at[sem], w_recv.at[sem], same_core(x * 16 + y * 4 + z_hi)
            ).start()

    along(1, w_full.at[blocks[0], core, x_pos, y_pos], 1)
    along(0, w_full.at[blocks[1], core, x_pos, y_pos], 2)

    carry = scan(states, 1)

    y_near = []
    for half in range(2):
        chunks = slice(half * CHIPS, (half + 1) * CHIPS)
        parts = range(half * CHIPS // 2, (half + 1) * CHIPS // 2)
        high, low = split(carry[chunks])
        for channel in range(OWN):
            value = y_rows[channel, chunks, :] + (
                matmul(high, back_high[1, channel])
                + (matmul(high, back_low[1, channel]) + matmul(low, back_high[1, channel]))
            )
            o_rows[pl.ds(half * CHIPS * OWN + channel, CHIPS, stride=OWN), :] = value
        for part in parts:
            y_give[part] = o_rows[(2 * part + 1) * OWN : (2 * part + 2) * OWN, :]
        piece = pl.ds(half * CHIPS // 2, CHIPS // 2)
        copy = remote(
            y_give.at[piece],
            y_take.at[piece],
            near_send.at[2 + half],
            near_recv.at[2 + half],
            sibling,
        )
        copy.start()
        y_near.append(copy)
    for half in (1, 0):
        y_near[1 - half].wait_recv()
        for part in range(half * CHIPS // 2, (half + 1) * CHIPS // 2):
            place = part + core * (CHIPS - 1 - 2 * part)
            total = o_rows[2 * part * OWN : (2 * part + 1) * OWN, :] + y_take[CHIPS - 1 - part]
            y_out[place] = total.astype(BF16)
    for step in STEPS:
        other = moved(step)
        remote(
            y_out.at[other], y_in.at[chip], out_send, out_recv.at[x_pos], same_core(other)
        ).start()
    y_in[chip] = y_out[chip]

    for half in range(2):
        wait_bytes(w_full.at[blocks[half], 0, 0, pl.ds(0, 3)], w_recv.at[1 + half])
    along(0, w_full.at[blocks[0], core, x_pos], 3)
    along(1, w_full.at[blocks[1], core, :, y_pos], 4)

    for offset in range(TILES):
        tile = lax.rem(x_pos + offset, TILES)
        wait_bytes(y_in.at[pl.ds(0, 15 if offset == 0 else 16)], out_recv.at[tile])
        for part in range(16):
            mix_f32[part * OWN : (part + 1) * OWN, :] = (
                y_in[tile * 16 + part].astype(F32)
                * post_t[tile, part * OWN : (part + 1) * OWN, :]
            )
        rows = pl.ds(pl.multiple_of(tile * LANES, LANES), LANES)
        mix[tp, rows, :] = mix_f32[...].astype(BF16)
        part = mix.at[tp, rows]
        remote(part, part, mix_send, mix_recv.at[2 + tile], {"tp": tp_peers[1]}).start()
        remote(part, part, mix_send, mix_recv.at[0], {"tp": tp_peers[0]}).start()

    for half in range(2):
        wait_bytes(w_full.at[blocks[half], 0, pl.ds(0, 3)], w_recv.at[3 + half])
    part = w_full.at[:, core]
    w_half = remote(part, part, w_send.at[5], w_recv.at[5], sibling)
    w_half.start()

    def project(block):
        return matmul(w_full[block].reshape(WIDTH, WIDTH), mix[block])

    w_half.wait_recv()
    acc[...] = project(tp)
    for offset in range(TILES):
        tile = lax.rem(x_pos + offset, TILES)
        part = mix.at[tp_peers[1], pl.ds(pl.multiple_of(tile * LANES, LANES), LANES)]
        wait_bytes(part, mix_recv.at[2 + tile])
        remote(part, part, mix_send, mix_recv.at[1], {"tp": tp_peers[0]}).start()
    acc[...] += project(tp_peers[1])
    wait_bytes(mix.at[tp_peers[0]], mix_recv.at[0])
    acc[...] += project(tp_peers[0])
    wait_bytes(mix.at[tp_peers[2]], mix_recv.at[1])
    acc[...] += project(tp_peers[2])
    for group in range(CHIPS):
        for part in range(2):
            first = part * (WIDTH // 2) + group * 4
            sums[group * 8 + part * 4 : group * 8 + part * 4 + 4, :] = acc[first : first + 4, :]
    for tile in range(TILES):
        rows = slice(tile * LANES, (tile + 1) * LANES)
        out_ref[:, rows] = sums[rows, :].T.astype(BF16)

    par_copy.wait_send()
    wait_bytes(v_in.at[pl.ds(0, CHIPS - 1), 0], v_send)
    wait_bytes(g_in.at[pl.ds(0, CHIPS - 1), 0], g_send)
    v_near.wait_send()
    g_near.wait_send()
    for copy in y_near:
        copy.wait_send()
    wait_bytes(y_in.at[pl.ds(0, CHIPS - 1)], out_send)
    wait_bytes(w_planes.at[pl.ds(0, 3)], w_send.at[0])
    for half in range(2):
        wait_bytes(w_full.at[blocks[half], 0, 0, pl.ds(0, 3)], w_send.at[1 + half])
        wait_bytes(w_full.at[blocks[half], 0, pl.ds(0, 3)], w_send.at[3 + half])
    w_half.wait_send()
    wait_bytes(mix.at[pl.ds(0, TP - 1)], mix_send)


def local(x_gate, x_post, values, decay, residue, w_out):
    dma = pltpu.SemaphoreType.DMA
    scratch = [
        pltpu.VMEM((CHUNK, WIDTH), BF16),
        pltpu.VMEM((CHUNK, WIDTH), BF16),
        pltpu.VMEM((CHUNK, WIDTH), BF16),
        pltpu.VMEM((2, POLES, WIDTH), F32),
        pltpu.VMEM((2, POLES, WIDTH), F32),
        pltpu.VMEM((4, TP * WIDTH), BF16),
        pltpu.VMEM((8, LANES), F32),
        pltpu.VMEM((8, LANES), F32),
        pltpu.VMEM((8, LANES), F32),
        pltpu.VMEM((CHIPS, OWN, CHUNK), BF16),
        pltpu.VMEM((CHIPS, OWN, CHUNK), BF16),
        pltpu.VMEM((CHIPS, 2, OWN, CHUNK), BF16),
        pltpu.VMEM((CHIPS, 2, OWN, CHUNK), BF16),
        pltpu.VMEM((CHUNKS * OWN, CHUNK), F32),
        pltpu.VMEM((CHUNKS * OWN, CHUNK), F32),
        pltpu.VMEM((TILES, LANES, CHUNK), F32),
        pltpu.VMEM((2, OWN, CHUNK, 2 * LANES), BF16),
        pltpu.VMEM((2, OWN, CHUNK, 2 * LANES), BF16),
        pltpu.VMEM((2, OWN, LANES, CHUNK), BF16),
        pltpu.VMEM((2, OWN, LANES, CHUNK), BF16),
        pltpu.VMEM((2, 8, LANES), F32),
        pltpu.VMEM((OWN, CHUNKS, CHUNK), F32),
        pltpu.VMEM((CHUNKS * OWN, CHUNK), F32),
        pltpu.VMEM((CHIPS, OWN, CHUNK), F32),
        pltpu.VMEM((CHIPS, OWN, CHUNK), F32),
        pltpu.VMEM((CHIPS, OWN, CHUNK), BF16),
        pltpu.VMEM((CHIPS, OWN, CHUNK), BF16),
        pltpu.VMEM((4, 4, TP * WIDTH), BF16),
        pltpu.VMEM((16, TP * WIDTH), F32),
        pltpu.VMEM((TP, 2, 4, 4, 16, WIDTH), BF16),
        pltpu.VMEM((LANES, CHUNK), F32),
        pltpu.VMEM((TP, WIDTH, CHUNK), BF16),
        pltpu.VMEM((WIDTH, CHUNK), F32),
        pltpu.VMEM((WIDTH, CHUNK), F32),
        dma((6,)),
        dma,
        dma,
        dma,
        dma,
        dma,
        dma,
        dma((4,)),
        dma((4,)),
        dma,
        dma((TILES,)),
        dma((6,)),
        dma((6,)),
        dma,
        dma((2 + TILES,)),
    ]
    return pl.pallas_call(
        mixer_kernel,
        out_shape=jax.ShapeDtypeStruct((CHUNK, WIDTH), BF16),
        in_specs=[pl.BlockSpec(memory_space=pl.ANY)] * 6,
        out_specs=pl.BlockSpec(memory_space=pltpu.VMEM),
        scratch_shapes=scratch,
        compiler_params=pltpu.CompilerParams(
            collective_id=0, has_side_effects=True, vmem_limit_bytes=48 * 1024 * 1024
        ),
        name="mixer",
    )(
        *(
            pltpu.with_memory_space_constraint(array, pltpu.HBM)
            for array in (
                x_gate,
                x_post,
                values,
                jnp.swapaxes(decay, 1, 2),
                jnp.swapaxes(residue, 1, 2),
                w_out,
            )
        )
    )


def solution(mesh):
    in_specs = (
        P("ctx", "tp"),
        P("ctx", "tp"),
        P("ctx", "tp"),
        P(None, "tp", None),
        P(None, "tp", None),
        P(("tp", "ctx"), None),
    )
    return jax.shard_map(
        local, mesh=mesh, in_specs=in_specs, out_specs=P("ctx", "tp"), check_vma=False
    )
```

```python
import jax
import jax.numpy as jnp
from jax import lax
from jax.experimental import pallas as pl
from jax.experimental.pallas import tpu as pltpu
from jax.sharding import PartitionSpec as P

MESH = pl.DeviceIdType.MESH
F32 = jnp.float32
BF16 = jnp.bfloat16
HIGHEST = lax.Precision.HIGHEST

POLES = 16
CHUNK = 128
CHUNKS = 128
CHIPS = 64
OWN = 8
LANES = 128
TILES = 4
TP = 4
WIDTH = TILES * LANES


def far_first():
    def hops(step):
        x, y, z = (min(part, 4 - part) for part in step)
        return x + y + 4 * z

    steps = [(x, y, z) for x in range(4) for y in range(4) for z in range(4)]
    return sorted(steps[1:], key=hops, reverse=True)


STEPS = far_first()


def split(value):
    high = value.astype(BF16)
    return high, (value - high.astype(F32)).astype(BF16)


def matmul(left, right):
    return jnp.dot(left, right, preferred_element_type=F32)


def product3(left, right_high, right_low):
    high, low = split(left)
    return matmul(high, right_high) + (matmul(high, right_low) + matmul(low, right_high))


def mixer_kernel(
    gate_hbm,
    post_hbm,
    vals_hbm,
    decay_hbm,
    residue_hbm,
    w_hbm,
    out_ref,
    gate_s,
    post_s,
    vals_s,
    decay_s,
    residue_s,
    w_s,
    par_own,
    par_out,
    par_in,
    v_out,
    g_out,
    v_in,
    g_in,
    v_rows,
    g_rows,
    post_t,
    table_high,
    table_low,
    back_high,
    back_low,
    rates,
    y_rows,
    o_rows,
    y_give,
    y_take,
    y_out,
    y_in,
    w_planes,
    w_block,
    w_full,
    mix_f32,
    mix,
    acc,
    sums,
    load_sem,
    par_send,
    par_recv,
    v_send,
    v_recv,
    g_send,
    g_recv,
    near_send,
    near_recv,
    out_send,
    out_recv,
    w_send,
    w_recv,
    mix_send,
    mix_recv,
):
    ctx = lax.axis_index("ctx")
    tp = lax.axis_index("tp")
    core = lax.rem(ctx, 2)
    chip = ctx // 2
    z_hi = lax.rem(chip, 4)
    y_pos = lax.rem(chip // 4, 4)
    x_pos = chip // 16
    plane = chip // 4
    sibling = {"ctx": ctx + 1 - 2 * core}
    tp_peers = (tp + 1 - 2 * lax.rem(tp, 2), lax.rem(tp + 2, TP), TP - 1 - tp)

    def moved(step):
        x = lax.rem(x_pos + step[0], 4)
        y = lax.rem(y_pos + step[1], 4)
        z = lax.rem(z_hi + step[2], 4)
        return x * 16 + y * 4 + z

    def same_core(other_chip):
        return {"ctx": other_chip * 2 + core}

    def remote(src, dst, send_sem, recv_sem, device):
        return pltpu.make_async_remote_copy(
            src_ref=src,
            dst_ref=dst,
            send_sem=send_sem,
            recv_sem=recv_sem,
            device_id=device,
            device_id_type=MESH,
        )

    def wait_bytes(ref, sem):
        pltpu.make_async_copy(ref, ref, sem).wait()

    loads = [
        pltpu.make_async_copy(src, dst, load_sem.at[index])
        for index, (src, dst) in enumerate(
            [
                (vals_hbm, vals_s),
                (gate_hbm, gate_s),
                (decay_hbm, decay_s),
                (residue_hbm, residue_s),
                (w_hbm, w_s),
                (post_hbm, post_s),
            ]
        )
    ]
    barrier = pltpu.get_barrier_semaphore()
    for step in STEPS:
        pl.semaphore_signal(
            barrier, inc=1, device_id=same_core(moved(step)), device_id_type=MESH
        )
    for other in tp_peers:
        pl.semaphore_signal(barrier, inc=1, device_id={"tp": other}, device_id_type=MESH)
    pl.semaphore_signal(barrier, inc=1, device_id=sibling, device_id_type=MESH)
    for load in loads:
        load.start()

    def spread(source, target):
        for tile in range(TILES):
            columns = source[:, tile * LANES : (tile + 1) * LANES].astype(F32).T
            for part in range(LANES // OWN):
                target[tile * 16 + part] = columns[part * OWN : (part + 1) * OWN].astype(BF16)

    loads[0].wait()
    spread(vals_s, v_out)
    loads[1].wait()
    spread(gate_s, g_out)

    row_id = lax.broadcasted_iota(jnp.int32, (WIDTH, LANES), 0)
    own_id = lax.broadcasted_iota(jnp.int32, (WIDTH, LANES), 1) // POLES + chip * OWN
    picks = jnp.concatenate(
        [(row_id == own_id).astype(F32), (row_id == WIDTH - 1 - own_id).astype(F32)], axis=1
    )
    pole_mask = (
        lax.broadcasted_iota(jnp.int32, (2, POLES, LANES), 1)
        == lax.rem(lax.broadcasted_iota(jnp.int32, (2, POLES, LANES), 2), POLES)
    ).astype(F32)
    loads[2].wait()
    loads[3].wait()
    par_out[...] = jnp.zeros((8, LANES), F32)
    par_own[...] = jnp.zeros((8, LANES), F32)
    for which, source in enumerate((decay_s, residue_s)):
        both = lax.dot_general(
            source[...].reshape(2 * POLES, WIDTH),
            picks,
            (((1,), (0,)), ((), ())),
            precision=HIGHEST,
            preferred_element_type=F32,
        )
        for target, part in ((par_own, both[:, :LANES]), (par_out, both[:, LANES:])):
            rows = jnp.sum(part.reshape(2, POLES, LANES) * pole_mask, axis=1)
            target[2 * which : 2 * which + 2, :] = rows
    loads[4].wait()
    w_planes[z_hi] = w_s[...]

    pl.semaphore_wait(barrier, len(STEPS) + (TP - 1) + 1)

    par_copy = remote(par_out, par_in, par_send, par_recv, {"tp": TP - 1 - tp})
    par_copy.start()
    for step in STEPS:
        other = moved(step)
        remote(v_out.at[other], v_in.at[chip, core], v_send, v_recv, same_core(other)).start()
    v_in[chip, core] = v_out[chip]

    for step in STEPS:
        other = moved(step)
        remote(g_out.at[other], g_in.at[chip, core], g_send, g_recv, same_core(other)).start()
    g_in[chip, core] = g_out[chip]

    for offset in (2, 1, 3):
        other = plane * 4 + lax.rem(z_hi + offset, 4)
        remote(
            w_planes.at[z_hi], w_planes.at[z_hi], w_send.at[0], w_recv.at[0], same_core(other)
        ).start()

    par_copy.wait_recv()
    poles = jnp.where(core == 1, par_in[...], par_own[...])
    square = (LANES, LANES)
    row = lax.broadcasted_iota(jnp.int32, square, 0)
    col = lax.broadcasted_iota(jnp.int32, square, 1)
    row_f = row.astype(F32)
    reverse = core == 1
    tap_power = jnp.where(reverse, jnp.where(row == 0, 0.0, CHUNK - row_f), row_f)
    out_power = jnp.where(reverse, CHUNK - row_f, row_f + 1.0)
    state_power = jnp.where(reverse, row_f, CHUNK - 1.0 - row_f)
    causal = (col - row) * (1 - 2 * core) >= 0
    channel_mask = (
        lax.broadcasted_iota(jnp.int32, (OWN, LANES), 1) // POLES
        == lax.broadcasted_iota(jnp.int32, (OWN, LANES), 0)
    ).astype(F32)

    def build(filt):
        decay = poles[filt : filt + 1, :]
        weight = poles[2 + filt : 3 + filt, :] * jnp.sqrt(2.0 * decay / POLES)
        rates[filt, 0:1, :] = decay
        taps = lax.dot_general(
            channel_mask,
            weight * jnp.exp(-decay * tap_power),
            (((1,), (1,)), ((), ())),
            precision=HIGHEST,
            preferred_element_type=F32,
        )
        to_states = jnp.exp(-decay * state_power)
        from_states = (weight * jnp.exp(-decay * out_power)).T
        for channel in range(OWN):
            line = jnp.broadcast_to(taps[channel : channel + 1, :], square)
            toeplitz = pltpu.roll(line, 0, 1, stride=1, stride_axis=0)
            high, low = split(jnp.where(causal, toeplitz, 0.0))
            table_high[filt, channel, :, :LANES] = high
            table_low[filt, channel, :, :LANES] = low
            high, low = split(jnp.where(col // POLES == channel, to_states, 0.0))
            table_high[filt, channel, :, LANES:] = high
            table_low[filt, channel, :, LANES:] = low
            high, low = split(jnp.where(row // POLES == channel, from_states, 0.0))
            back_high[filt, channel] = high
            back_low[filt, channel] = low

    build(0)
    build(1)
    loads[5].wait()
    for tile in range(TILES):
        post_t[tile] = post_s[:, tile * LANES : (tile + 1) * LANES].astype(F32).T

    def gather_rows(source, target):
        def body(other, done):
            for half in range(2):
                chunk = other * 2 + half
                place = chunk + core * (CHUNKS - 1 - 2 * chunk)
                rows = pl.ds(pl.multiple_of(place * OWN, OWN), OWN)
                target[rows, :] = source[other, half].astype(F32)
            return done

        lax.fori_loop(0, CHIPS, body, 0, unroll=8)

    def picked(ref, channel):
        return ref[pl.ds(channel, CHUNKS, stride=OWN), :]

    def near(ref, index):
        part = ref.at[:, core]
        return remote(part, part, near_send.at[index], near_recv.at[index], sibling)

    def scan(states, filt):
        decay = rates[filt, 0:1, :]

        def later(value, count):
            return jnp.where(row >= count, pltpu.roll(value, count, 0), 0.0)

        value = later(states, 1)
        for power in range(7):
            count = 2**power
            value = value + jnp.exp(-float(CHUNK * count) * decay) * later(value, count)
        return value

    wait_bytes(v_in.at[pl.ds(0, CHIPS - 1), 0], v_recv)
    v_near = near(v_in, 0)
    v_near.start()
    v_near.wait_recv()
    gather_rows(v_in, v_rows)

    states = jnp.zeros(square, F32)
    for channel in range(OWN):
        line = picked(v_rows, channel).astype(BF16)
        both = matmul(line, table_high[0, channel]) + matmul(line, table_low[0, channel])
        y_rows[channel] = both[:, :LANES]
        states = states + both[:, LANES:]
    carry = scan(states, 0)
    wait_bytes(g_in.at[pl.ds(0, CHIPS - 1), 0], g_recv)
    g_near = near(g_in, 1)
    g_near.start()

    g_near.wait_recv()
    gather_rows(g_in, g_rows)

    states = jnp.zeros(square, F32)
    for channel in range(OWN):
        value = y_rows[channel] + product3(carry, back_high[0, channel], back_low[0, channel])
        value = value * picked(g_rows, channel)
        both = product3(value, table_high[1, channel], table_low[1, channel])
        y_rows[channel] = both[:, :LANES]
        states = states + both[:, LANES:]
    wait_bytes(w_planes.at[pl.ds(0, 3)], w_recv.at[0])
    for other in range(4):
        w_block[other * 4 : other * 4 + 4, :] = w_planes[other].astype(F32)
    for block in range(TP):
        columns = slice(block * WIDTH, (block + 1) * WIDTH)
        w_full[block, core, x_pos, y_pos] = w_block[:, columns].astype(BF16)
    blocks = (pl.ds(0, 2), pl.ds(2, 2))

    def along(axis, part, sem):
        for offset in (2, 1, 3):
            x = lax.rem(x_pos + offset, 4) if axis == 0 else x_pos
            y = lax.rem(y_pos + offset, 4) if axis == 1 else y_pos
            remote(
                part, part, w_send.at[sem], w_recv.at[sem], same_core(x * 16 + y * 4 + z_hi)
            ).start()

    along(1, w_full.at[blocks[0], core, x_pos, y_pos], 1)
    along(0, w_full.at[blocks[1], core, x_pos, y_pos], 2)

    carry = scan(states, 1)

    y_near = []
    for half in range(2):
        chunks = slice(half * CHIPS, (half + 1) * CHIPS)
        parts = range(half * CHIPS // 2, (half + 1) * CHIPS // 2)
        high, low = split(carry[chunks])
        for channel in range(OWN):
            value = y_rows[channel, chunks, :] + (
                matmul(high, back_high[1, channel])
                + (matmul(high, back_low[1, channel]) + matmul(low, back_high[1, channel]))
            )
            o_rows[pl.ds(half * CHIPS * OWN + channel, CHIPS, stride=OWN), :] = value
        for part in parts:
            given = o_rows[(2 * part + 1) * OWN : (2 * part + 2) * OWN, :]
            y_give[part] = given.astype(BF16)
        piece = pl.ds(half * CHIPS // 2, CHIPS // 2)
        copy = remote(
            y_give.at[piece],
            y_take.at[piece],
            near_send.at[2 + half],
            near_recv.at[2 + half],
            sibling,
        )
        copy.start()
        y_near.append(copy)
    for half in (1, 0):
        y_near[1 - half].wait_recv()
        for part in range(half * CHIPS // 2, (half + 1) * CHIPS // 2):
            place = part + core * (CHIPS - 1 - 2 * part)
            kept = o_rows[2 * part * OWN : (2 * part + 1) * OWN, :]
            total = kept + y_take[CHIPS - 1 - part].astype(F32)
            y_out[place] = total.astype(BF16)
    for step in STEPS:
        other = moved(step)
        remote(
            y_out.at[other], y_in.at[chip], out_send, out_recv.at[x_pos], same_core(other)
        ).start()
    y_in[chip] = y_out[chip]

    for half in range(2):
        wait_bytes(w_full.at[blocks[half], 0, 0, pl.ds(0, 3)], w_recv.at[1 + half])
    along(0, w_full.at[blocks[0], core, x_pos], 3)
    along(1, w_full.at[blocks[1], core, :, y_pos], 4)

    for offset in (0, 1, 3, 2):
        tile = lax.rem(x_pos + offset, TILES)
        wait_bytes(y_in.at[pl.ds(0, 15 if offset == 0 else 16)], out_recv.at[tile])
        for part in range(16):
            mix_f32[part * OWN : (part + 1) * OWN, :] = (
                y_in[tile * 16 + part].astype(F32)
                * post_t[tile, part * OWN : (part + 1) * OWN, :]
            )
        rows = pl.ds(pl.multiple_of(tile * LANES, LANES), LANES)
        mix[tp, rows, :] = mix_f32[...].astype(BF16)
        part = mix.at[tp, rows]
        remote(part, part, mix_send, mix_recv.at[2 + tile], {"tp": tp_peers[1]}).start()
        remote(part, part, mix_send, mix_recv.at[0], {"tp": tp_peers[0]}).start()

    for half in range(2):
        wait_bytes(w_full.at[blocks[half], 0, pl.ds(0, 3)], w_recv.at[3 + half])
    part = w_full.at[:, core]
    w_half = remote(part, part, w_send.at[5], w_recv.at[5], sibling)
    w_half.start()

    def project(block):
        return matmul(w_full[block].reshape(WIDTH, WIDTH), mix[block])

    w_half.wait_recv()
    acc[...] = project(tp)
    for offset in (0, 1, 3, 2):
        tile = lax.rem(x_pos + offset, TILES)
        part = mix.at[tp_peers[1], pl.ds(pl.multiple_of(tile * LANES, LANES), LANES)]
        wait_bytes(part, mix_recv.at[2 + tile])
        remote(part, part, mix_send, mix_recv.at[1], {"tp": tp_peers[0]}).start()
    acc[...] += project(tp_peers[1])
    wait_bytes(mix.at[tp_peers[0]], mix_recv.at[0])
    acc[...] += project(tp_peers[0])
    wait_bytes(mix.at[tp_peers[2]], mix_recv.at[1])
    acc[...] += project(tp_peers[2])
    for group in range(CHIPS):
        for part in range(2):
            first = part * (WIDTH // 2) + group * 4
            sums[group * 8 + part * 4 : group * 8 + part * 4 + 4, :] = acc[first : first + 4, :]
    for tile in range(TILES):
        rows = slice(tile * LANES, (tile + 1) * LANES)
        out_ref[:, rows] = sums[rows, :].T.astype(BF16)

    par_copy.wait_send()
    wait_bytes(v_in.at[pl.ds(0, CHIPS - 1), 0], v_send)
    wait_bytes(g_in.at[pl.ds(0, CHIPS - 1), 0], g_send)
    v_near.wait_send()
    g_near.wait_send()
    for copy in y_near:
        copy.wait_send()
    wait_bytes(y_in.at[pl.ds(0, CHIPS - 1)], out_send)
    wait_bytes(w_planes.at[pl.ds(0, 3)], w_send.at[0])
    for half in range(2):
        wait_bytes(w_full.at[blocks[half], 0, 0, pl.ds(0, 3)], w_send.at[1 + half])
        wait_bytes(w_full.at[blocks[half], 0, pl.ds(0, 3)], w_send.at[3 + half])
    w_half.wait_send()
    wait_bytes(mix.at[pl.ds(0, TP - 1)], mix_send)


def local(x_gate, x_post, values, decay, residue, w_out):
    dma = pltpu.SemaphoreType.DMA
    scratch = [
        pltpu.VMEM((CHUNK, WIDTH), BF16),
        pltpu.VMEM((CHUNK, WIDTH), BF16),
        pltpu.VMEM((CHUNK, WIDTH), BF16),
        pltpu.VMEM((2, POLES, WIDTH), F32),
        pltpu.VMEM((2, POLES, WIDTH), F32),
        pltpu.VMEM((4, TP * WIDTH), BF16),
        pltpu.VMEM((8, LANES), F32),
        pltpu.VMEM((8, LANES), F32),
        pltpu.VMEM((8, LANES), F32),
        pltpu.VMEM((CHIPS, OWN, CHUNK), BF16),
        pltpu.VMEM((CHIPS, OWN, CHUNK), BF16),
        pltpu.VMEM((CHIPS, 2, OWN, CHUNK), BF16),
        pltpu.VMEM((CHIPS, 2, OWN, CHUNK), BF16),
        pltpu.VMEM((CHUNKS * OWN, CHUNK), F32),
        pltpu.VMEM((CHUNKS * OWN, CHUNK), F32),
        pltpu.VMEM((TILES, LANES, CHUNK), F32),
        pltpu.VMEM((2, OWN, CHUNK, 2 * LANES), BF16),
        pltpu.VMEM((2, OWN, CHUNK, 2 * LANES), BF16),
        pltpu.VMEM((2, OWN, LANES, CHUNK), BF16),
        pltpu.VMEM((2, OWN, LANES, CHUNK), BF16),
        pltpu.VMEM((2, 8, LANES), F32),
        pltpu.VMEM((OWN, CHUNKS, CHUNK), F32),
        pltpu.VMEM((CHUNKS * OWN, CHUNK), F32),
        pltpu.VMEM((CHIPS, OWN, CHUNK), BF16),
        pltpu.VMEM((CHIPS, OWN, CHUNK), BF16),
        pltpu.VMEM((CHIPS, OWN, CHUNK), BF16),
        pltpu.VMEM((CHIPS, OWN, CHUNK), BF16),
        pltpu.VMEM((4, 4, TP * WIDTH), BF16),
        pltpu.VMEM((16, TP * WIDTH), F32),
        pltpu.VMEM((TP, 2, 4, 4, 16, WIDTH), BF16),
        pltpu.VMEM((LANES, CHUNK), F32),
        pltpu.VMEM((TP, WIDTH, CHUNK), BF16),
        pltpu.VMEM((WIDTH, CHUNK), F32),
        pltpu.VMEM((WIDTH, CHUNK), F32),
        dma((6,)),
        dma,
        dma,
        dma,
        dma,
        dma,
        dma,
        dma((4,)),
        dma((4,)),
        dma,
        dma((TILES,)),
        dma((6,)),
        dma((6,)),
        dma,
        dma((2 + TILES,)),
    ]
    return pl.pallas_call(
        mixer_kernel,
        out_shape=jax.ShapeDtypeStruct((CHUNK, WIDTH), BF16),
        in_specs=[pl.BlockSpec(memory_space=pl.ANY)] * 6,
        out_specs=pl.BlockSpec(memory_space=pltpu.VMEM),
        scratch_shapes=scratch,
        compiler_params=pltpu.CompilerParams(
            collective_id=0, has_side_effects=True, vmem_limit_bytes=48 * 1024 * 1024
        ),
        name="mixer",
    )(
        *(
            pltpu.with_memory_space_constraint(array, pltpu.HBM)
            for array in (
                x_gate,
                x_post,
                values,
                jnp.swapaxes(decay, 1, 2),
                jnp.swapaxes(residue, 1, 2),
                w_out,
            )
        )
    )


def solution(mesh):
    in_specs = (
        P("ctx", "tp"),
        P("ctx", "tp"),
        P("ctx", "tp"),
        P(None, "tp", None),
        P(None, "tp", None),
        P(("tp", "ctx"), None),
    )
    return jax.shard_map(
        local, mesh=mesh, in_specs=in_specs, out_specs=P("ctx", "tp"), check_vma=False
    )
```

```python
import jax
import jax.numpy as jnp
from jax import lax
from jax.experimental import pallas as pl
from jax.experimental.pallas import tpu as pltpu
from jax.sharding import PartitionSpec as P

MESH = pl.DeviceIdType.MESH
F32 = jnp.float32
BF16 = jnp.bfloat16
HIGHEST = lax.Precision.HIGHEST

POLES = 16
CHUNK = 128
CHUNKS = 128
CHIPS = 64
OWN = 8
LANES = 128
TILES = 4
TP = 4
WIDTH = TILES * LANES


def far_first():
    def hops(step):
        x, y, z = (min(part, 4 - part) for part in step)
        return x + y + 4 * z

    steps = [(x, y, z) for x in range(4) for y in range(4) for z in range(4)]
    return sorted(steps[1:], key=hops, reverse=True)


STEPS = far_first()


def split(value):
    high = value.astype(BF16)
    return high, (value - high.astype(F32)).astype(BF16)


def matmul(left, right):
    return jnp.dot(left, right, preferred_element_type=F32)


def product3(left, right_high, right_low):
    high, low = split(left)
    return matmul(high, right_high) + (matmul(high, right_low) + matmul(low, right_high))


def mixer_kernel(
    gate_hbm,
    post_hbm,
    vals_hbm,
    decay_hbm,
    residue_hbm,
    w_hbm,
    out_ref,
    gate_s,
    post_s,
    vals_s,
    decay_s,
    residue_s,
    w_s,
    par_own,
    par_out,
    par_in,
    v_out,
    g_out,
    v_in,
    g_in,
    v_rows,
    g_rows,
    post_t,
    table_high,
    table_low,
    back_high,
    back_low,
    rates,
    y_rows,
    o_rows,
    y_give,
    y_take,
    y_out,
    y_in,
    w_planes,
    w_block,
    w_full,
    mix_f32,
    mix,
    acc,
    sums,
    load_sem,
    par_send,
    par_recv,
    v_send,
    v_recv,
    g_send,
    g_recv,
    near_send,
    near_recv,
    out_send,
    out_recv,
    w_send,
    w_recv,
    mix_send,
    mix_recv,
):
    ctx = lax.axis_index("ctx")
    tp = lax.axis_index("tp")
    core = lax.rem(ctx, 2)
    chip = ctx // 2
    z_hi = lax.rem(chip, 4)
    y_pos = lax.rem(chip // 4, 4)
    x_pos = chip // 16
    plane = chip // 4
    sibling = {"ctx": ctx + 1 - 2 * core}
    tp_peers = (tp + 1 - 2 * lax.rem(tp, 2), lax.rem(tp + 2, TP), TP - 1 - tp)

    def moved(step):
        x = lax.rem(x_pos + step[0], 4)
        y = lax.rem(y_pos + step[1], 4)
        z = lax.rem(z_hi + step[2], 4)
        return x * 16 + y * 4 + z

    def same_core(other_chip):
        return {"ctx": other_chip * 2 + core}

    def remote(src, dst, send_sem, recv_sem, device):
        return pltpu.make_async_remote_copy(
            src_ref=src,
            dst_ref=dst,
            send_sem=send_sem,
            recv_sem=recv_sem,
            device_id=device,
            device_id_type=MESH,
        )

    def wait_bytes(ref, sem):
        pltpu.make_async_copy(ref, ref, sem).wait()

    loads = [
        pltpu.make_async_copy(src, dst, load_sem.at[index])
        for index, (src, dst) in enumerate(
            [
                (vals_hbm, vals_s),
                (gate_hbm, gate_s),
                (decay_hbm, decay_s),
                (residue_hbm, residue_s),
                (w_hbm, w_s),
                (post_hbm, post_s),
            ]
        )
    ]
    barrier = pltpu.get_barrier_semaphore()
    for step in STEPS:
        pl.semaphore_signal(
            barrier, inc=1, device_id=same_core(moved(step)), device_id_type=MESH
        )
    for other in tp_peers:
        pl.semaphore_signal(barrier, inc=1, device_id={"tp": other}, device_id_type=MESH)
    pl.semaphore_signal(barrier, inc=1, device_id=sibling, device_id_type=MESH)
    for load in loads:
        load.start()

    def spread(source, target):
        for tile in range(TILES):
            columns = source[:, tile * LANES : (tile + 1) * LANES].astype(F32).T
            for part in range(LANES // OWN):
                target[tile * 16 + part] = columns[part * OWN : (part + 1) * OWN].astype(BF16)

    loads[0].wait()
    spread(vals_s, v_out)
    loads[1].wait()
    spread(gate_s, g_out)

    row_id = lax.broadcasted_iota(jnp.int32, (WIDTH, LANES), 0)
    own_id = lax.broadcasted_iota(jnp.int32, (WIDTH, LANES), 1) // POLES + chip * OWN
    picks = jnp.concatenate(
        [(row_id == own_id).astype(F32), (row_id == WIDTH - 1 - own_id).astype(F32)], axis=1
    )
    pole_mask = (
        lax.broadcasted_iota(jnp.int32, (2, POLES, LANES), 1)
        == lax.rem(lax.broadcasted_iota(jnp.int32, (2, POLES, LANES), 2), POLES)
    ).astype(F32)
    loads[2].wait()
    loads[3].wait()
    par_out[...] = jnp.zeros((8, LANES), F32)
    par_own[...] = jnp.zeros((8, LANES), F32)
    for which, source in enumerate((decay_s, residue_s)):
        both = lax.dot_general(
            source[...].reshape(2 * POLES, WIDTH),
            picks,
            (((1,), (0,)), ((), ())),
            precision=HIGHEST,
            preferred_element_type=F32,
        )
        for target, part in ((par_own, both[:, :LANES]), (par_out, both[:, LANES:])):
            rows = jnp.sum(part.reshape(2, POLES, LANES) * pole_mask, axis=1)
            target[2 * which : 2 * which + 2, :] = rows
    loads[4].wait()
    w_planes[z_hi] = w_s[...]

    pl.semaphore_wait(barrier, len(STEPS) + (TP - 1) + 1)

    par_copy = remote(par_out, par_in, par_send, par_recv, {"tp": TP - 1 - tp})
    par_copy.start()
    for step in STEPS:
        other = moved(step)
        remote(v_out.at[other], v_in.at[chip, core], v_send, v_recv, same_core(other)).start()
    v_in[chip, core] = v_out[chip]

    for step in STEPS:
        other = moved(step)
        remote(g_out.at[other], g_in.at[chip, core], g_send, g_recv, same_core(other)).start()
    g_in[chip, core] = g_out[chip]

    for offset in (2, 1, 3):
        other = plane * 4 + lax.rem(z_hi + offset, 4)
        remote(
            w_planes.at[z_hi], w_planes.at[z_hi], w_send.at[0], w_recv.at[0], same_core(other)
        ).start()

    par_copy.wait_recv()
    poles = jnp.where(core == 1, par_in[...], par_own[...])
    square = (LANES, LANES)
    row = lax.broadcasted_iota(jnp.int32, square, 0)
    col = lax.broadcasted_iota(jnp.int32, square, 1)
    row_f = row.astype(F32)
    reverse = core == 1
    tap_power = jnp.where(reverse, jnp.where(row == 0, 0.0, CHUNK - row_f), row_f)
    out_power = jnp.where(reverse, CHUNK - row_f, row_f + 1.0)
    state_power = jnp.where(reverse, row_f, CHUNK - 1.0 - row_f)
    causal = (col - row) * (1 - 2 * core) >= 0
    channel_mask = (
        lax.broadcasted_iota(jnp.int32, (OWN, LANES), 1) // POLES
        == lax.broadcasted_iota(jnp.int32, (OWN, LANES), 0)
    ).astype(F32)

    def build(filt):
        decay = poles[filt : filt + 1, :]
        weight = poles[2 + filt : 3 + filt, :] * jnp.sqrt(2.0 * decay / POLES)
        rates[filt, 0:1, :] = decay
        taps = lax.dot_general(
            channel_mask,
            weight * jnp.exp(-decay * tap_power),
            (((1,), (1,)), ((), ())),
            precision=HIGHEST,
            preferred_element_type=F32,
        )
        to_states = jnp.exp(-decay * state_power)
        from_states = (weight * jnp.exp(-decay * out_power)).T
        for channel in range(OWN):
            line = jnp.broadcast_to(taps[channel : channel + 1, :], square)
            toeplitz = pltpu.roll(line, 0, 1, stride=1, stride_axis=0)
            high, low = split(jnp.where(causal, toeplitz, 0.0))
            table_high[filt, channel, :, :LANES] = high
            table_low[filt, channel, :, :LANES] = low
            high, low = split(jnp.where(col // POLES == channel, to_states, 0.0))
            table_high[filt, channel, :, LANES:] = high
            table_low[filt, channel, :, LANES:] = low
            high, low = split(jnp.where(row // POLES == channel, from_states, 0.0))
            back_high[filt, channel] = high
            back_low[filt, channel] = low

    build(0)
    build(1)
    loads[5].wait()
    for tile in range(TILES):
        post_t[tile] = post_s[:, tile * LANES : (tile + 1) * LANES].astype(F32).T

    def gather_rows(source, target):
        def body(other, done):
            for half in range(2):
                chunk = other * 2 + half
                place = chunk + core * (CHUNKS - 1 - 2 * chunk)
                rows = pl.ds(pl.multiple_of(place * OWN, OWN), OWN)
                target[rows, :] = source[other, half].astype(F32)
            return done

        lax.fori_loop(0, CHIPS, body, 0, unroll=8)

    def picked(ref, channel):
        return ref[pl.ds(channel, CHUNKS, stride=OWN), :]

    def near(ref, index):
        part = ref.at[:, core]
        return remote(part, part, near_send.at[index], near_recv.at[index], sibling)

    def scan(states, filt):
        decay = rates[filt, 0:1, :]

        def later(value, count):
            return jnp.where(row >= count, pltpu.roll(value, count, 0), 0.0)

        value = later(states, 1)
        for power in range(7):
            count = 2**power
            value = value + jnp.exp(-float(CHUNK * count) * decay) * later(value, count)
        return value

    wait_bytes(v_in.at[pl.ds(0, CHIPS - 1), 0], v_recv)
    v_near = near(v_in, 0)
    v_near.start()
    v_near.wait_recv()
    gather_rows(v_in, v_rows)

    states = jnp.zeros(square, F32)
    for channel in range(OWN):
        line = picked(v_rows, channel).astype(BF16)
        both = matmul(line, table_high[0, channel]) + matmul(line, table_low[0, channel])
        y_rows[channel] = both[:, :LANES]
        states = states + both[:, LANES:]
    carry = scan(states, 0)
    wait_bytes(g_in.at[pl.ds(0, CHIPS - 1), 0], g_recv)
    g_near = near(g_in, 1)
    g_near.start()

    g_near.wait_recv()
    gather_rows(g_in, g_rows)

    states = jnp.zeros(square, F32)
    for channel in range(OWN):
        value = y_rows[channel] + product3(carry, back_high[0, channel], back_low[0, channel])
        value = value * picked(g_rows, channel)
        both = product3(value, table_high[1, channel], table_low[1, channel])
        y_rows[channel] = both[:, :LANES]
        states = states + both[:, LANES:]
    wait_bytes(w_planes.at[pl.ds(0, 3)], w_recv.at[0])
    for other in range(4):
        w_block[other * 4 : other * 4 + 4, :] = w_planes[other].astype(F32)
    for block in range(TP):
        columns = slice(block * WIDTH, (block + 1) * WIDTH)
        w_full[block, core, x_pos, y_pos] = w_block[:, columns].astype(BF16)
    blocks = (pl.ds(0, 2), pl.ds(2, 2))

    def along(axis, part, sem):
        for offset in (2, 1, 3):
            x = lax.rem(x_pos + offset, 4) if axis == 0 else x_pos
            y = lax.rem(y_pos + offset, 4) if axis == 1 else y_pos
            remote(
                part, part, w_send.at[sem], w_recv.at[sem], same_core(x * 16 + y * 4 + z_hi)
            ).start()

    along(1, w_full.at[blocks[0], core, x_pos, y_pos], 1)
    along(0, w_full.at[blocks[1], core, x_pos, y_pos], 2)

    carry = scan(states, 1)

    y_near = []
    for half in range(2):
        chunks = slice(half * CHIPS, (half + 1) * CHIPS)
        parts = range(half * CHIPS // 2, (half + 1) * CHIPS // 2)
        high, low = split(carry[chunks])
        for channel in range(OWN):
            value = y_rows[channel, chunks, :] + (
                matmul(high, back_high[1, channel])
                + (matmul(high, back_low[1, channel]) + matmul(low, back_high[1, channel]))
            )
            o_rows[pl.ds(half * CHIPS * OWN + channel, CHIPS, stride=OWN), :] = value
        for part in parts:
            y_give[part] = o_rows[(2 * part + 1) * OWN : (2 * part + 2) * OWN, :]
        piece = pl.ds(half * CHIPS // 2, CHIPS // 2)
        copy = remote(
            y_give.at[piece],
            y_take.at[piece],
            near_send.at[2 + half],
            near_recv.at[2 + half],
            sibling,
        )
        copy.start()
        y_near.append(copy)
    for half in (1, 0):
        y_near[1 - half].wait_recv()
        for part in range(half * CHIPS // 2, (half + 1) * CHIPS // 2):
            place = part + core * (CHIPS - 1 - 2 * part)
            total = o_rows[2 * part * OWN : (2 * part + 1) * OWN, :] + y_take[CHIPS - 1 - part]
            y_out[place] = total.astype(BF16)
    for step in STEPS:
        other = moved(step)
        remote(
            y_out.at[other], y_in.at[chip], out_send, out_recv.at[x_pos], same_core(other)
        ).start()
    y_in[chip] = y_out[chip]

    for half in range(2):
        wait_bytes(w_full.at[blocks[half], 0, 0, pl.ds(0, 3)], w_recv.at[1 + half])
    along(0, w_full.at[blocks[0], core, x_pos], 3)
    along(1, w_full.at[blocks[1], core, :, y_pos], 4)

    for offset in range(TILES):
        tile = lax.rem(x_pos + offset, TILES)
        wait_bytes(y_in.at[pl.ds(0, 15 if offset == 0 else 16)], out_recv.at[tile])
        for part in range(16):
            mix_f32[part * OWN : (part + 1) * OWN, :] = (
                y_in[tile * 16 + part].astype(F32)
                * post_t[tile, part * OWN : (part + 1) * OWN, :]
            )
        rows = pl.ds(pl.multiple_of(tile * LANES, LANES), LANES)
        mix[tp, rows, :] = mix_f32[...].astype(BF16)
        part = mix.at[tp, rows]
        remote(part, part, mix_send, mix_recv.at[2 + tile], {"tp": tp_peers[1]}).start()
        remote(part, part, mix_send, mix_recv.at[0], {"tp": tp_peers[0]}).start()

    for half in range(2):
        wait_bytes(w_full.at[blocks[half], 0, pl.ds(0, 3)], w_recv.at[3 + half])
    part = w_full.at[:, core]
    w_half = remote(part, part, w_send.at[5], w_recv.at[5], sibling)
    w_half.start()

    def project(block):
        return matmul(w_full[block].reshape(WIDTH, WIDTH), mix[block])

    for offset in range(TILES):
        tile = lax.rem(x_pos + offset, TILES)
        part = mix.at[tp_peers[1], pl.ds(pl.multiple_of(tile * LANES, LANES), LANES)]
        wait_bytes(part, mix_recv.at[2 + tile])
        remote(part, part, mix_send, mix_recv.at[1], {"tp": tp_peers[0]}).start()
    w_half.wait_recv()
    acc[...] = project(tp)
    acc[...] += project(tp_peers[1])
    wait_bytes(mix.at[tp_peers[0]], mix_recv.at[0])
    acc[...] += project(tp_peers[0])
    wait_bytes(mix.at[tp_peers[2]], mix_recv.at[1])
    acc[...] += project(tp_peers[2])
    for group in range(CHIPS):
        for part in range(2):
            first = part * (WIDTH // 2) + group * 4
            sums[group * 8 + part * 4 : group * 8 + part * 4 + 4, :] = acc[first : first + 4, :]
    for tile in range(TILES):
        rows = slice(tile * LANES, (tile + 1) * LANES)
        out_ref[:, rows] = sums[rows, :].T.astype(BF16)

    par_copy.wait_send()
    wait_bytes(v_in.at[pl.ds(0, CHIPS - 1), 0], v_send)
    wait_bytes(g_in.at[pl.ds(0, CHIPS - 1), 0], g_send)
    v_near.wait_send()
    g_near.wait_send()
    for copy in y_near:
        copy.wait_send()
    wait_bytes(y_in.at[pl.ds(0, CHIPS - 1)], out_send)
    wait_bytes(w_planes.at[pl.ds(0, 3)], w_send.at[0])
    for half in range(2):
        wait_bytes(w_full.at[blocks[half], 0, 0, pl.ds(0, 3)], w_send.at[1 + half])
        wait_bytes(w_full.at[blocks[half], 0, pl.ds(0, 3)], w_send.at[3 + half])
    w_half.wait_send()
    wait_bytes(mix.at[pl.ds(0, TP - 1)], mix_send)


def local(x_gate, x_post, values, decay, residue, w_out):
    dma = pltpu.SemaphoreType.DMA
    scratch = [
        pltpu.VMEM((CHUNK, WIDTH), BF16),
        pltpu.VMEM((CHUNK, WIDTH), BF16),
        pltpu.VMEM((CHUNK, WIDTH), BF16),
        pltpu.VMEM((2, POLES, WIDTH), F32),
        pltpu.VMEM((2, POLES, WIDTH), F32),
        pltpu.VMEM((4, TP * WIDTH), BF16),
        pltpu.VMEM((8, LANES), F32),
        pltpu.VMEM((8, LANES), F32),
        pltpu.VMEM((8, LANES), F32),
        pltpu.VMEM((CHIPS, OWN, CHUNK), BF16),
        pltpu.VMEM((CHIPS, OWN, CHUNK), BF16),
        pltpu.VMEM((CHIPS, 2, OWN, CHUNK), BF16),
        pltpu.VMEM((CHIPS, 2, OWN, CHUNK), BF16),
        pltpu.VMEM((CHUNKS * OWN, CHUNK), F32),
        pltpu.VMEM((CHUNKS * OWN, CHUNK), F32),
        pltpu.VMEM((TILES, LANES, CHUNK), F32),
        pltpu.VMEM((2, OWN, CHUNK, 2 * LANES), BF16),
        pltpu.VMEM((2, OWN, CHUNK, 2 * LANES), BF16),
        pltpu.VMEM((2, OWN, LANES, CHUNK), BF16),
        pltpu.VMEM((2, OWN, LANES, CHUNK), BF16),
        pltpu.VMEM((2, 8, LANES), F32),
        pltpu.VMEM((OWN, CHUNKS, CHUNK), F32),
        pltpu.VMEM((CHUNKS * OWN, CHUNK), F32),
        pltpu.VMEM((CHIPS, OWN, CHUNK), F32),
        pltpu.VMEM((CHIPS, OWN, CHUNK), F32),
        pltpu.VMEM((CHIPS, OWN, CHUNK), BF16),
        pltpu.VMEM((CHIPS, OWN, CHUNK), BF16),
        pltpu.VMEM((4, 4, TP * WIDTH), BF16),
        pltpu.VMEM((16, TP * WIDTH), F32),
        pltpu.VMEM((TP, 2, 4, 4, 16, WIDTH), BF16),
        pltpu.VMEM((LANES, CHUNK), F32),
        pltpu.VMEM((TP, WIDTH, CHUNK), BF16),
        pltpu.VMEM((WIDTH, CHUNK), F32),
        pltpu.VMEM((WIDTH, CHUNK), F32),
        dma((6,)),
        dma,
        dma,
        dma,
        dma,
        dma,
        dma,
        dma((4,)),
        dma((4,)),
        dma,
        dma((TILES,)),
        dma((6,)),
        dma((6,)),
        dma,
        dma((2 + TILES,)),
    ]
    return pl.pallas_call(
        mixer_kernel,
        out_shape=jax.ShapeDtypeStruct((CHUNK, WIDTH), BF16),
        in_specs=[pl.BlockSpec(memory_space=pl.ANY)] * 6,
        out_specs=pl.BlockSpec(memory_space=pltpu.VMEM),
        scratch_shapes=scratch,
        compiler_params=pltpu.CompilerParams(
            collective_id=0, has_side_effects=True, vmem_limit_bytes=48 * 1024 * 1024
        ),
        name="mixer",
    )(
        *(
            pltpu.with_memory_space_constraint(array, pltpu.HBM)
            for array in (
                x_gate,
                x_post,
                values,
                jnp.swapaxes(decay, 1, 2),
                jnp.swapaxes(residue, 1, 2),
                w_out,
            )
        )
    )


def solution(mesh):
    in_specs = (
        P("ctx", "tp"),
        P("ctx", "tp"),
        P("ctx", "tp"),
        P(None, "tp", None),
        P(None, "tp", None),
        P(("tp", "ctx"), None),
    )
    return jax.shard_map(
        local, mesh=mesh, in_specs=in_specs, out_specs=P("ctx", "tp"), check_vma=False
    )
```
